32 devices in a mesh: row: 16 (over z, y, core), col: 2 (over x).
Axes of the slice: x: 2, y: 2, z: 4, core: 2. Of those that a mesh axis runs over, the one named last changes fastest.
Arguments:
- anchor: bfloat16 [4096, 128], P(('row', 'col')), may hold values from -3 to 3
- injection: bfloat16 [4096, 128], P(('row', 'col')), may hold values from -6 to 6
- weight: bfloat16 [128, 128], replicated, may hold values from -0.25 to 0.25
- cotangent: bfloat16 [4096, 128], P(('row', 'col')), may hold values from -6 to 6
- node_mask: int32 [4096], P(('row', 'col')), may hold values 0 or 1
- tile_values: bfloat16 [16, 2, 64, 128, 128], P('row', 'col'), may hold values from -0.09375 to 0.09375
- tile_rows: int32 [16, 2, 64], P('row', 'col'), may hold values from 0 to 1
- tile_cols: int32 [16, 2, 64], P('row', 'col'), may hold values from 0 to 15
- tile_counts: int32 [16, 2], P('row', 'col'), may hold values from 1 to 64, as said below
Outputs:
- state: bfloat16 [4096, 128], P(('row', 'col'))
- adjoint: float32 [4096, 128], P(('row', 'col'))
- weight_grad: float32 [128, 128], replicated
The draws below stay inside these ranges and needn't reach their ends.
Inputs may be any that keep to these rules, and one draw needn't show every extreme that they name: Slot k of device (r, c) is live exactly when k < tile_counts[r, c]; some device has all 64 slots live in every draw.
All inputs are finite; a program needn't handle non-finite values. No bound on the sum of `node_mask` on one device may be relied on, other than what follows from the above.
Results may differ from the reference program's by a relative error of at most 0.006.
Values may be sent and summed in bfloat16 or wider, within the bound.
No kernel may reach another device: no remote copies, remote signals or barrier semaphores. Data moves between devices by JAX's collectives and lax.ppermute only.
A program may use at most 64 MiB of HBM per device.

```python
import jax
import jax.numpy as jnp
from jax import lax

H = 128
TILE = 128
NODE_DEV = 128
CAP = 64
ITERS = 3
ADJOINT = 3
NODES = 4096
TILE_ROWS = 2
TILE_COLS = 16
N_ROW = 16
N_COL = 2


def draw_tile_counts(key, part):
    first_key, second_key, spot_key = jax.random.split(jax.random.fold_in(key, 17), 3)
    first = jax.random.randint(first_key, (N_ROW * N_COL,), 1, 9)
    second = jax.random.randint(second_key, (N_ROW * N_COL,), 1, 9)
    counts = jnp.maximum(CAP * first * second // 64, 1)
    spot = jax.random.randint(spot_key, (), 0, N_ROW * N_COL)
    places = jnp.arange(N_ROW * N_COL)
    counts = jnp.where(places == spot, CAP, counts)
    return counts.reshape(N_ROW, N_COL).astype(jnp.int32)


def with_ends(result, key, low, high):
    longest = result.shape.index(max(result.shape))
    spots = []
    for shift in (0, 1):
        where = [jax.random.randint(jax.random.fold_in(key, axis), (), 0, length) for axis, length in enumerate(result.shape)]
        where[longest] = (where[longest] + shift) % result.shape[longest]
        spots.append(tuple(where))
    return result.at[spots[0]].set(low).at[spots[1]].set(high)


def steps_of(stream_key, dims, cuts, low, high):
    def one(dim, shards_of):
        steps = jax.random.uniform(jax.random.fold_in(jax.random.fold_in(stream_key, 6), dim), (shards_of,), jnp.float32, low / len(cuts), high / len(cuts))
        return jnp.repeat(jnp.exp(steps), dims[dim] // shards_of).reshape((-1,) + (1,) * (len(dims) - dim - 1))

    factor_of = one(*cuts[0])
    for cut in cuts[1:]:
        factor_of = factor_of * one(*cut)
    return factor_of


def bell_draw(key, shape, width, reach, cuts=(), kind=jnp.bfloat16):
    result = jax.random.normal(key, shape, jnp.float32) * width
    if len(cuts) > 0:
        result = steps_of(key, shape, cuts, -0.22, 0.18) * result
    return jnp.clip(result, min=-reach, max=reach).astype(kind)


def setup_inputs(seed: int = 0) -> dict:
    keys = jax.random.split(jax.random.key(seed), 10)
    return {
        "anchor": bell_draw(keys[0], (NODES, H), 0.5, 3.0, ((0, 32),)),
        "injection": bell_draw(keys[1], (NODES, H), 1.0, 6.0, ((0, 32),)),
        "weight": bell_draw(keys[2], (H, H), (4 * H) ** -0.5, 0.25),
        "cotangent": bell_draw(keys[3], (NODES, H), 1.0, 6.0, ((0, 32),)),
        "node_mask": with_ends((jax.random.randint(keys[4], (NODES,), 0, 4) < 3).astype(jnp.int32), jax.random.fold_in(keys[4], 1), 0, 1),
        "tile_values": bell_draw(keys[5], (N_ROW, N_COL, CAP, TILE, TILE), (CAP * 128 // TILE_ROWS) ** -0.5, 0.09375, ((0, 16), (1, 2))),
        "tile_rows": with_ends(jax.random.randint(keys[6], (N_ROW, N_COL, CAP), 0, TILE_ROWS), jax.random.fold_in(keys[6], 1), 0, TILE_ROWS - 1).astype(jnp.int32),
        "tile_cols": with_ends(jax.random.randint(keys[7], (N_ROW, N_COL, CAP), 0, TILE_COLS), jax.random.fold_in(keys[7], 1), 0, TILE_COLS - 1).astype(jnp.int32),
        "tile_counts": draw_tile_counts(jax.random.fold_in(keys[9], 71), 0),
    }


def spread(tile_rows, tile_cols, tile_counts):
    rank_row = jnp.arange(N_ROW, dtype=jnp.int32)[:, None, None]
    rank_col = jnp.arange(N_COL, dtype=jnp.int32)[None, :, None]
    row_start = rank_row * (N_COL * NODE_DEV) + tile_rows * TILE
    local = tile_cols * TILE
    col_start = ((local // NODE_DEV) * N_COL + rank_col) * NODE_DEV + local % NODE_DEV
    slots = jnp.arange(CAP, dtype=jnp.int32)[None, None, :]
    live = (slots < tile_counts[:, :, None]).astype(jnp.float32)
    return row_start.reshape(-1, CAP), col_start.reshape(-1, CAP), live.reshape(-1, CAP)


def tile_product(source, tile_values, row_start, col_start, live, transpose):
    offsets = jnp.arange(TILE, dtype=jnp.int32)

    def step(total, item):
        tiles, starts_row, starts_col, alive = item
        row_index = (starts_row[:, None] + offsets[None, :]).astype(jnp.int32)
        col_index = (starts_col[:, None] + offsets[None, :]).astype(jnp.int32)
        blocks = tiles.astype(jnp.float32)
        if transpose:
            pieces = source[row_index].astype(jnp.float32)
            product = jnp.einsum("kij,kih->kjh", blocks, pieces) * alive[:, None, None]
            total = total.at[col_index].add(product)
        else:
            pieces = source[col_index].astype(jnp.float32)
            product = jnp.einsum("kij,kjh->kih", blocks, pieces) * alive[:, None, None]
            total = total.at[row_index].add(product)
        return total, None

    start = jnp.zeros(source.shape, jnp.float32)
    items = (tile_values.reshape(-1, CAP, TILE, TILE), row_start, col_start, live)
    total, _ = lax.scan(step, start, items)
    return total


def reference(anchor, injection, weight, cotangent, node_mask, tile_values, tile_rows, tile_cols, tile_counts):
    row_start, col_start, live = spread(tile_rows, tile_cols, tile_counts)
    anchor_f = anchor.astype(jnp.float32)
    inject_f = injection.astype(jnp.float32)
    state = anchor
    last_pre = inject_f
    last_state = anchor
    for step in range(ITERS):
        projected = jnp.dot(state, weight, preferred_element_type=jnp.float32).astype(jnp.bfloat16)
        pre = tile_product(projected, tile_values, row_start, col_start, live, False) + inject_f
        beta = 1.0 / (step + 2.0)
        last_pre = pre
        last_state = state
        state = (beta * anchor_f + (1.0 - beta) * jnp.tanh(pre)).astype(jnp.bfloat16)
    slope = 1.0 - jnp.tanh(last_pre) ** 2
    masked_grad = cotangent.astype(jnp.float32) * node_mask.astype(jnp.float32)[:, None]
    adjoint = masked_grad
    pulled = masked_grad
    weight_f = weight.astype(jnp.float32)
    for step in range(ADJOINT):
        scaled = (adjoint * slope).astype(jnp.bfloat16)
        pulled = tile_product(scaled, tile_values, row_start, col_start, live, True)
        adjoint = masked_grad + jnp.dot(pulled, weight_f.T, precision=lax.Precision.HIGHEST)
    weight_grad = jnp.dot(last_state.astype(jnp.float32).T, pulled, precision=lax.Precision.HIGHEST) / (NODE_DEV * N_COL)
    return state, adjoint, weight_grad
```

```python
import jax
import jax.numpy as jnp
from jax import lax
from jax.experimental import pallas as pl
from jax.experimental.pallas import tpu as pltpu
from jax.sharding import PartitionSpec as P

TILE = 128
ITERS = 3
ADJOINT = 3
BF16 = jnp.bfloat16
F32 = jnp.float32
VMEM_LIMIT = 48 * 2**20


def vmem_call(body, outs, *args, smem=0, scratch=()):
    specs = [
        pl.BlockSpec(memory_space=pltpu.SMEM if i < smem else pltpu.VMEM) for i in range(len(args))
    ]
    out_specs = [pl.BlockSpec(memory_space=pltpu.VMEM) for _ in outs]
    return pl.pallas_call(
        body,
        out_shape=[jax.ShapeDtypeStruct(shape, dtype) for shape, dtype in outs],
        in_specs=specs,
        out_specs=out_specs,
        scratch_shapes=list(scratch),
        compiler_params=pltpu.CompilerParams(vmem_limit_bytes=VMEM_LIMIT),
    )(*args)


def split_dot(value, factor, dims):
    high = value.astype(BF16)
    low = (value - high.astype(F32)).astype(BF16)
    return lax.dot_general(high, factor, (dims, ((), ())), preferred_element_type=F32) + lax.dot_general(
        low, factor, (dims, ((), ())), preferred_element_type=F32
    )


def per_device(n_row, n_col, *args):
    anchor, injection, weight, cotangent, node_mask, tile_values, tile_rows, tile_cols, tile_counts = args
    own, hidden = anchor.shape
    assert own == TILE
    slots = tile_values.shape[2]
    me_row = lax.axis_index("row")
    me_col = lax.axis_index("col")
    z_step = n_row // 4
    y_steps = [1 << b for b in range(1, z_step.bit_length() - 1)]
    half = n_row // 2

    def exchange(value, axis, distance):
        size = n_row if axis == "row" else n_col
        return lax.ppermute(value, axis, [(i, i ^ distance) for i in range(size)])

    order = [z * z_step for z in range(4)]
    for step in y_steps + [1]:
        order = order + [s ^ step for s in order]

    def position(s):
        place = s // z_step
        weight_of = 4
        for step in y_steps + [1]:
            place = place + ((s // step) % 2) * weight_of
            weight_of *= 2
        return place

    def build(where, rows, cols, count, tiles, a_out, at_out, acc):
        acc[...] = jnp.zeros_like(acc)

        def add(k, carry):
            place = position(cols[k] ^ where[0])
            row = rows[k] ^ where[1]
            acc[row * n_row + place] += tiles[k].astype(F32)
            return carry

        lax.fori_loop(0, count[0], add, 0)

        def finish(p, carry):
            for row in range(n_col):
                tile = acc[row * n_row + p]
                lanes = pl.ds(pl.multiple_of(p * TILE, TILE), TILE)
                a_out[row * TILE : (row + 1) * TILE, lanes] = tile.astype(BF16)
                at_out[lanes, row * TILE : (row + 1) * TILE] = tile.T.astype(BF16)
            return carry

        lax.fori_loop(0, n_row, finish, 0)

    where = jnp.stack([me_row, me_col]).astype(jnp.int32)
    adjacency, adjacency_t = vmem_call(
        build,
        [((n_col * TILE, n_row * TILE), BF16), ((n_row * TILE, n_col * TILE), BF16)],
        where,
        tile_rows.reshape(-1),
        tile_cols.reshape(-1),
        tile_counts.reshape(-1),
        tile_values.reshape(slots, TILE, TILE),
        smem=4,
        scratch=[pltpu.VMEM((n_col * n_row, TILE, TILE), F32)],
    )
    masked_grad = cotangent.astype(F32) * node_mask.astype(F32)[:, None]

    def gather_rows(block):
        line = jnp.concatenate(
            [block] + [exchange(block, "row", z * z_step) for z in (1, 2, 3)], axis=0
        )
        for step in y_steps:
            line = jnp.concatenate([line, exchange(line, "row", step)], axis=0)
        return line, exchange(line, "row", 1)

    def forward_partial(near, far, a, *outs):
        cut = half * TILE
        total = jnp.dot(a[:, :cut], near[...], preferred_element_type=F32)
        total += jnp.dot(a[:, cut:], far[...], preferred_element_type=F32)
        outs[0][...] = total[:TILE]
        if n_col > 1:
            outs[1][...] = total[TILE:].astype(BF16)

    def reduce_cols(mine, rest):
        parts = [mine] + [rest[i * TILE : (i + 1) * TILE] for i in range(n_col - 1)]
        step = n_col // 2
        while step > 1:
            send = jnp.concatenate([p.astype(BF16) for p in parts[step : 2 * step]], axis=0)
            got = exchange(send, "col", step)
            parts = [
                parts[i].astype(F32) + got[i * TILE : (i + 1) * TILE].astype(F32) for i in range(step)
            ]
            step //= 2
        return parts[0], exchange(parts[1].astype(BF16), "col", 1)

    def advance(beta, last):
        def body(mine, got, w, anchor_ref, inject, *rest):
            u = mine[...] + got[...].astype(F32)
            pre = split_dot(u, w[...], ((1,), (0,))) + inject[...].astype(F32)
            bent = jnp.tanh(pre)
            outs = rest[1:] if last else rest
            outs[0][...] = (beta * anchor_ref[...].astype(F32) + (1.0 - beta) * bent).astype(BF16)
            if last:
                slope = 1.0 - bent * bent
                outs[1][...] = slope
                outs[2][...] = u
                outs[3][...] = (rest[0][...] * slope).astype(BF16)

        return body

    block = (TILE, hidden)
    state = anchor
    for step in range(ITERS):
        near, far = gather_rows(state)
        outs = [(block, F32), (((n_col - 1) * TILE, hidden), BF16)]
        mine, rest = vmem_call(forward_partial, outs, near, far, adjacency)
        mine, got = reduce_cols(mine, rest)
        beta = 1.0 / (step + 2.0)
        inputs = (mine, got, weight, anchor, injection)
        if step < ITERS - 1:
            (state,) = vmem_call(advance(beta, False), [(block, BF16)], *inputs)
        else:
            state, slope, mixed, scaled = vmem_call(
                advance(beta, True),
                [(block, BF16), (block, F32), (block, F32), (block, BF16)],
                *inputs,
                masked_grad,
            )

    def outer(u, h, out):
        out[...] = split_dot(u[...], h[...], ((0,), (0,)))

    def backward_partial(h, a_t, near, far):
        cut = half * TILE
        near[...] = jnp.dot(a_t[:cut], h[...], preferred_element_type=F32)
        far[...] = jnp.dot(a_t[cut:], h[...], preferred_element_type=F32).astype(BF16)

    def fold(kept, blocks):
        def body(held, got, keep, send):
            cut = blocks * TILE
            keep[...] = held[:cut] + got[:cut].astype(F32)
            send[...] = (held[cut : 2 * cut] + got[cut : 2 * cut].astype(F32)).astype(BF16)

        return body

    def pull(last):
        def body(held, got, r1, r2, r3, base, w, slope_ref, *outs):
            v = (held[...] + r1[...].astype(F32)) + (r2[...].astype(F32) + r3[...].astype(F32))
            g = base[...] + split_dot(v, w[...], ((1,), (1,)))
            outs[0][...] = g if last else (g * slope_ref[...]).astype(BF16)

        return body

    def gather_cols(value):
        step = 1
        while step < n_col:
            value = jnp.concatenate([value, exchange(value, "col", step)], axis=0)
            step *= 2
        return value

    for step in range(ADJOINT):
        last = step == ADJOINT - 1
        if last:
            (term,) = vmem_call(outer, [((hidden, hidden), F32)], mixed, scaled)
        block_states = gather_cols(scaled)
        near, far = vmem_call(
            backward_partial,
            [((half * TILE, hidden), F32), ((half * TILE, hidden), BF16)],
            block_states,
            adjacency_t,
        )
        held = near
        got = exchange(far, "row", 1)
        blocks = half
        for y_step in reversed(y_steps):
            blocks //= 2
            held, send = vmem_call(
                fold(held, blocks),
                [((blocks * TILE, hidden), F32), ((blocks * TILE, hidden), BF16)],
                held,
                got,
            )
            got = exchange(send, "row", y_step)
        total = held + got.astype(F32)
        parts = [total[i * TILE : (i + 1) * TILE] for i in range(4)]
        came = [exchange(parts[z].astype(BF16), "row", z * z_step) for z in (1, 2, 3)]
        (result,) = vmem_call(
            pull(last),
            [(block, F32 if last else BF16)],
            parts[0],
            parts[0],
            *came,
            masked_grad,
            weight,
            slope,
        )
        scaled = result
    adjoint = result

    col_steps = [1 << b for b in range(n_col.bit_length() - 1)]
    for axis, distance in [("col", s) for s in col_steps] + [("row", s) for s in [1] + y_steps]:
        term = term + exchange(term, axis, distance)
    others = [exchange(term, "row", z * z_step) for z in (1, 2, 3)]
    weight_grad = ((term + others[0]) + (others[1] + others[2])) / (own * n_col)
    return state, adjoint, weight_grad


def solution(mesh):
    in_specs = (
        P(("row", "col"), None),
        P(("row", "col"), None),
        P(),
        P(("row", "col"), None),
        P(("row", "col")),
        P("row", "col", None, None, None),
        P("row", "col", None),
        P("row", "col", None),
        P("row", "col"),
    )
    out_specs = (P(("row", "col"), None), P(("row", "col"), None), P())

    def whole(*args):
        return per_device(mesh.shape["row"], mesh.shape["col"], *args)

    return jax.shard_map(whole, mesh=mesh, in_specs=in_specs, out_specs=out_specs, check_vma=False)
```

```python
import jax
import jax.numpy as jnp
from jax import lax
from jax.experimental import pallas as pl
from jax.experimental.pallas import tpu as pltpu
from jax.sharding import PartitionSpec as P

TILE = 128
ITERS = 3
ADJOINT = 3
LINE = 4
BF16 = jnp.bfloat16
F32 = jnp.float32
VMEM_LIMIT = 48 * 2**20


def vmem_call(body, outs, *args, smem=0, scratch=()):
    specs = [
        pl.BlockSpec(memory_space=pltpu.SMEM if i < smem else pltpu.VMEM) for i in range(len(args))
    ]
    out_specs = [pl.BlockSpec(memory_space=pltpu.VMEM) for _ in outs]
    return pl.pallas_call(
        body,
        out_shape=[jax.ShapeDtypeStruct(shape, dtype) for shape, dtype in outs],
        in_specs=specs,
        out_specs=out_specs,
        scratch_shapes=list(scratch),
        compiler_params=pltpu.CompilerParams(vmem_limit_bytes=VMEM_LIMIT),
    )(*args)


def halves(value):
    high = value.astype(BF16)
    return high, (value - high.astype(F32)).astype(BF16)


def split_dot(value, factor, dims):
    high, low = halves(value)
    return lax.dot_general(high, factor, (dims, ((), ())), preferred_element_type=F32) + lax.dot_general(
        low, factor, (dims, ((), ())), preferred_element_type=F32
    )


def tree_sum(values):
    while len(values) > 1:
        values = [values[i] + values[i + 1] for i in range(0, len(values), 2)]
    return values[0]


def per_device(n_row, n_col, *args):
    anchor, injection, weight, cotangent, node_mask, tile_values, tile_rows, tile_cols, tile_counts = args
    own, hidden = anchor.shape
    assert own == TILE
    slots = tile_values.shape[2]
    z_step = n_row // LINE
    n_y = z_step // 2
    square = [(y, x) for y in range(n_y) for x in range(n_col)]
    line_rows = LINE * TILE
    block = (TILE, hidden)
    where = jnp.stack([lax.axis_index("row"), lax.axis_index("col")]).astype(jnp.int32)

    def exchange(value, row_xor, col_xor=0):
        if col_xor == 0:
            return lax.ppermute(value, "row", [(i, i ^ row_xor) for i in range(n_row)])
        if row_xor == 0:
            return lax.ppermute(value, "col", [(i, i ^ col_xor) for i in range(n_col)])
        pairs = [
            (r * n_col + c, (r ^ row_xor) * n_col + (c ^ col_xor))
            for r in range(n_row)
            for c in range(n_col)
        ]
        return lax.ppermute(value, ("row", "col"), pairs)

    def along_line(values):
        return [exchange(v, z * z_step) for z, v in zip(range(1, LINE), values)]

    def to_square(values):
        return [exchange(v, 2 * y, x) for (y, x), v in zip(square[1:], values)]

    def build(where_ref, rows, cols, count, tiles, *refs):
        parts, turned, acc = refs[:n_y], refs[n_y], refs[n_y + 1]
        acc[...] = jnp.zeros_like(acc)

        def add(k, carry):
            s = cols[k] ^ where_ref[0]
            x = rows[k] ^ where_ref[1]
            y = (s // 2) % n_y
            acc[((y * n_col + x) * 2 + s % 2) * LINE + s // z_step] += tiles[k].astype(F32)
            return carry

        lax.fori_loop(0, count[0], add, 0)
        for y in range(n_y):
            for x in range(n_col):
                for p in range(2 * LINE):
                    tile = acc[(y * n_col + x) * 2 * LINE + p]
                    here, there = slice(x * TILE, (x + 1) * TILE), slice(p * TILE, (p + 1) * TILE)
                    parts[y][here, there] = tile.astype(BF16)
                    if y == 0:
                        turned[there, here] = tile.T.astype(BF16)

    part_shape = (n_col * TILE, 2 * line_rows)
    *parts, turned = vmem_call(
        build,
        [(part_shape, BF16)] * n_y + [(part_shape[::-1], BF16)],
        where,
        tile_rows.reshape(-1),
        tile_cols.reshape(-1),
        tile_counts.reshape(-1),
        tile_values.reshape(slots, TILE, TILE),
        smem=4,
        scratch=[pltpu.VMEM((n_y * n_col * 2 * LINE, TILE, TILE), F32)],
    )
    masked_grad = cotangent.astype(F32) * node_mask.astype(F32)[:, None]

    def first_partial(near, far, *refs):
        a, outs = refs[:n_y], refs[n_y:]
        total = jnp.zeros((n_col * TILE, hidden), F32)
        for y in range(n_y):
            rows = slice(y * line_rows, (y + 1) * line_rows)
            total += jnp.dot(a[y][:, :line_rows], near[rows], preferred_element_type=F32)
            total += jnp.dot(a[y][:, line_rows:], far[rows], preferred_element_type=F32)
        outs[0][...] = total[:TILE]
        for x in range(1, n_col):
            outs[x][...] = total[x * TILE : (x + 1) * TILE].astype(BF16)

    def forward_partial(z0, z1, z2, z3, far, *refs):
        a, outs = refs[:n_y], refs[n_y:]
        near = jnp.concatenate([z0[...], z1[...], z2[...], z3[...]], axis=0)
        for y in range(n_y):
            total = jnp.dot(a[y][:, :line_rows], near, preferred_element_type=F32)
            total += jnp.dot(a[y][:, line_rows:], far[...], preferred_element_type=F32)
            for x in range(n_col):
                out = outs[y * n_col + x]
                out[...] = total[x * TILE : (x + 1) * TILE].astype(out.dtype)

    def advance(beta, last, peers):
        def body(*refs):
            sums, (w, anchor_ref, inject), rest = refs[:peers], refs[peers : peers + 3], refs[peers + 3 :]
            u = tree_sum([s[...].astype(F32) for s in sums])
            pre = split_dot(u, w[...], ((1,), (0,))) + inject[...].astype(F32)
            bent = jnp.tanh(pre)
            outs = rest[1:] if last else rest
            outs[0][...] = (beta * anchor_ref[...].astype(F32) + (1.0 - beta) * bent).astype(BF16)
            if last:
                slope = 1.0 - bent * bent
                outs[1][...] = slope
                outs[2][...] = u
                outs[3][...] = (rest[0][...] * slope).astype(BF16)

        return body

    state = anchor
    for step in range(ITERS):
        line = [state] + along_line([state] * (LINE - 1))
        if step == 0:
            joined = jnp.concatenate(line, axis=0)
            joined, *parts, turned = lax.optimization_barrier((joined, *parts, turned))
            bit = 2
            while bit < z_step:
                joined = jnp.concatenate([joined, exchange(joined, bit)], axis=0)
                bit *= 2
            joined, *sent = lax.optimization_barrier((joined, *parts[1:]))
            far = exchange(joined, 1)
            outs = [(block, F32)] + [(block, BF16)] * (n_col - 1)
            mine, *sends = vmem_call(first_partial, outs, joined, far, *parts)
            parts = [parts[0]] + [exchange(p, 2 * (i + 1)) for i, p in enumerate(sent)]
            got = [exchange(v, 0, x + 1) for x, v in enumerate(sends)]
        else:
            far = exchange(jnp.concatenate(line, axis=0), 1)
            outs = [(block, F32)] + [(block, BF16)] * (len(square) - 1)
            mine, *sends = vmem_call(forward_partial, outs, *line, far, *parts)
            got = to_square(sends)
        last = step == ITERS - 1
        results = [(block, BF16)] + ([(block, F32), (block, F32), (block, BF16)] if last else [])
        state, *rest = vmem_call(
            advance(1.0 / (step + 2.0), last, 1 + len(got)),
            results,
            mine,
            *got,
            weight,
            anchor,
            injection,
            *([masked_grad] if last else []),
        )
    slope, mixed, scaled = rest

    def turn(*refs):
        for part, out in zip(refs[: n_y - 1], refs[n_y - 1 :]):
            for x in range(n_col):
                for p in range(2 * LINE):
                    here, there = slice(x * TILE, (x + 1) * TILE), slice(p * TILE, (p + 1) * TILE)
                    out[there, here] = part[here, there].T

    turned = [turned] + list(vmem_call(turn, [(part_shape[::-1], BF16)] * (n_y - 1), *parts[1:]))

    def backward_partial(last):
        def body(*refs):
            n = len(square)
            h, a_t, (near, far, *term) = refs[:n], refs[n : n + n_y], refs[n + n_y :]
            total = None
            for y in range(n_y):
                joined = jnp.concatenate([h[y * n_col + x][:TILE] for x in range(n_col)], axis=0)
                product = jnp.dot(a_t[y][...], joined, preferred_element_type=F32)
                total = product if total is None else total + product
            near[...] = total[:line_rows]
            far[:line_rows] = total[line_rows:].astype(BF16)
            if last:
                whole = tree_sum([v[TILE:].astype(F32) for v in h])
                high, low = halves(whole)
                far[line_rows : line_rows + hidden] = high
                far[line_rows + hidden :] = low
                term[0][...] = high.astype(F32) + low.astype(F32)

        return body

    def fold(last):
        def body(held, got, *refs):
            outs = refs[1:] if last else refs
            for z in range(LINE):
                rows = slice(z * TILE, (z + 1) * TILE)
                value = held[rows] + got[rows].astype(F32)
                if z == 0:
                    outs[0][...] = value
                else:
                    outs[z][:TILE] = value.astype(BF16)
            if last:
                high, low = got[line_rows : line_rows + hidden], got[line_rows + hidden :]
                term = (refs[0][...] + (high.astype(F32) + low.astype(F32))).astype(BF16)
                outs[LINE][...] = term.astype(F32)
                for z in range(1, LINE):
                    outs[z][TILE:] = term

        return body

    def pull(last, ride):
        def body(held, *refs):
            got, rest = refs[: LINE - 1], refs[LINE - 1 :]
            v = tree_sum([held[...]] + [r[:TILE].astype(F32) for r in got])
            base, w, slope_ref = rest[:3]
            g = base[...] + split_dot(v, w[...], ((1,), (1,)))
            if last:
                term, adjoint_out, grad_out = rest[3:]
                adjoint_out[...] = g
                whole = tree_sum([term[...]] + [r[TILE:].astype(F32) for r in got])
                grad_out[...] = whole / (own * n_col)
            else:
                out = rest[-1]
                h = (g * slope_ref[...]).astype(BF16)
                out[:TILE] = h
                if ride:
                    out[TILE:] = split_dot(rest[3][...], h, ((0,), (0,))).astype(BF16)

        return body

    for step in range(ADJOINT):
        last, ride = step == ADJOINT - 1, step == ADJOINT - 2
        states = [scaled] + to_square([scaled] * (len(square) - 1))
        extra = 2 * hidden if last else 0
        near, far, *term = vmem_call(
            backward_partial(last),
            [((line_rows, hidden), F32), ((line_rows + extra, hidden), BF16)]
            + ([((hidden, hidden), F32)] if last else []),
            *states,
            *turned,
        )
        got = exchange(far, 1)
        extra = hidden if last else 0
        held, *sends = vmem_call(
            fold(last),
            [(block, F32)]
            + [((TILE + extra, hidden), BF16)] * (LINE - 1)
            + ([((hidden, hidden), F32)] if last else []),
            near,
            got,
            *term,
        )
        if last:
            *sends, total = sends
        got = along_line(sends)
        inputs = (held, *got, masked_grad, weight, slope)
        if last:
            adjoint, weight_grad = vmem_call(
                pull(True, False), [(block, F32), ((hidden, hidden), F32)], *inputs, total
            )
        else:
            rows = TILE + (hidden if ride else 0)
            (scaled,) = vmem_call(
                pull(False, ride), [((rows, hidden), BF16)], *inputs, *([mixed] if ride else [])
            )
    return state, adjoint, weight_grad


def solution(mesh):
    in_specs = (
        P(("row", "col"), None),
        P(("row", "col"), None),
        P(),
        P(("row", "col"), None),
        P(("row", "col")),
        P("row", "col", None, None, None),
        P("row", "col", None),
        P("row", "col", None),
        P("row", "col"),
    )
    out_specs = (P(("row", "col"), None), P(("row", "col"), None), P())

    def whole(*args):
        return per_device(mesh.shape["row"], mesh.shape["col"], *args)

    return jax.shard_map(whole, mesh=mesh, in_specs=in_specs, out_specs=out_specs, check_vma=False)
```

```python
import jax
import jax.numpy as jnp
from jax import lax
from jax.experimental import pallas as pl
from jax.experimental.pallas import tpu as pltpu
from jax.sharding import PartitionSpec as P

TILE = 128
ITERS = 3
ADJOINT = 3
LINE = 4
BF16 = jnp.bfloat16
F32 = jnp.float32
VMEM_LIMIT = 48 * 2**20


def vmem_call(body, outs, *args, spaces=None, scratch=()):
    specs = [pl.BlockSpec(memory_space=space) for space in spaces or [pltpu.VMEM] * len(args)]
    out_specs = [pl.BlockSpec(memory_space=pltpu.VMEM) for _ in outs]
    return pl.pallas_call(
        body,
        out_shape=[jax.ShapeDtypeStruct(shape, dtype) for shape, dtype in outs],
        in_specs=specs,
        out_specs=out_specs,
        scratch_shapes=list(scratch),
        compiler_params=pltpu.CompilerParams(vmem_limit_bytes=VMEM_LIMIT),
    )(*args)


def halves(value):
    high = value.astype(BF16)
    return high, (value - high.astype(F32)).astype(BF16)


def split_dot(value, factor, dims):
    high, low = halves(value)
    return lax.dot_general(high, factor, (dims, ((), ())), preferred_element_type=F32) + lax.dot_general(
        low, factor, (dims, ((), ())), preferred_element_type=F32
    )


def tree_sum(values):
    while len(values) > 1:
        values = [values[i] + values[i + 1] for i in range(0, len(values), 2)]
    return values[0]


def per_device(n_row, n_col, *args):
    anchor, injection, weight, cotangent, node_mask, tile_values, tile_rows, tile_cols, tile_counts = args
    own, hidden = anchor.shape
    assert own == TILE
    slots = tile_values.shape[2]
    z_step = n_row // LINE
    n_y = z_step // 2
    square = [(y, x) for y in range(n_y) for x in range(n_col)]
    line_rows = LINE * TILE
    block = (TILE, hidden)
    where = jnp.stack([lax.axis_index("row"), lax.axis_index("col")]).astype(jnp.int32)

    def exchange(value, row_xor, col_xor=0):
        if col_xor == 0:
            return lax.ppermute(value, "row", [(i, i ^ row_xor) for i in range(n_row)])
        if row_xor == 0:
            return lax.ppermute(value, "col", [(i, i ^ col_xor) for i in range(n_col)])
        pairs = [
            (r * n_col + c, (r ^ row_xor) * n_col + (c ^ col_xor))
            for r in range(n_row)
            for c in range(n_col)
        ]
        return lax.ppermute(value, ("row", "col"), pairs)

    def along_line(values):
        return [exchange(v, z * z_step) for z, v in zip(range(1, LINE), values)]

    def to_square(values):
        return [exchange(v, 2 * y, x) for (y, x), v in zip(square[1:], values)]

    chunk = min(16, slots)
    n_chunks = slots // chunk
    assert slots % chunk == 0

    def build(where_ref, count, rows_hbm, cols_hbm, tiles_hbm, inject, cotan, mask, *refs):
        parts, turned, fixed_out = refs[:n_y], refs[n_y], refs[n_y + 1]
        rows, cols, tiles, acc, index_sem, tile_sem = refs[n_y + 2 :]
        copies = [
            pltpu.make_async_copy(rows_hbm, rows, index_sem.at[0]),
            pltpu.make_async_copy(cols_hbm, cols, index_sem.at[1]),
        ]
        pieces = [slice(c * chunk, (c + 1) * chunk) for c in range(n_chunks)]
        loads = [
            pltpu.make_async_copy(tiles_hbm.at[0, 0, piece], tiles.at[piece], tile_sem.at[c])
            for c, piece in enumerate(pieces)
        ]
        for copy in copies + loads:
            copy.start()
        acc[...] = jnp.zeros_like(acc)
        fixed_out[:TILE] = inject[...]
        kept_nodes = jnp.broadcast_to(mask[...].astype(F32), (TILE, TILE)).T[:, :1]
        fixed_out[TILE:] = (cotan[...].astype(F32) * kept_nodes).astype(BF16)
        for copy in copies:
            copy.wait()

        def add(k, carry):
            s = cols[0, 0, k] ^ where_ref[0]
            x = rows[0, 0, k] ^ where_ref[1]
            y = (s // 2) % n_y
            acc[((y * n_col + x) * 2 + s % 2) * LINE + s // z_step] += tiles[k].astype(F32)
            return carry

        for c, load in enumerate(loads):
            load.wait()
            lax.fori_loop(c * chunk, jnp.clip(count[0, 0], c * chunk, (c + 1) * chunk), add, 0)
        for y in range(n_y):
            for x in range(n_col):
                for p in range(2 * LINE):
                    tile = acc[(y * n_col + x) * 2 * LINE + p]
                    here, there = slice(x * TILE, (x + 1) * TILE), slice(p * TILE, (p + 1) * TILE)
                    parts[y][here, there] = tile.astype(BF16)
                    if y == 0:
                        turned[there, here] = tile.T.astype(BF16)
            if y > 0:
                parts[y][: 2 * TILE, 2 * line_rows :] = fixed_out[...]
                if n_col > 2:
                    parts[y][2 * TILE :, 2 * line_rows :] = jnp.zeros(((n_col - 2) * TILE, hidden), BF16)

    assert n_col >= 2
    part_shape = (n_col * TILE, 2 * line_rows)
    sent_shape = (n_col * TILE, 2 * line_rows + hidden)
    *parts, turned, fixed = vmem_call(
        build,
        [(part_shape, BF16)] + [(sent_shape, BF16)] * (n_y - 1)
        + [(part_shape[::-1], BF16), ((2 * TILE, hidden), BF16)],
        where,
        tile_counts,
        *[pltpu.with_memory_space_constraint(v, pltpu.HBM) for v in (tile_rows, tile_cols, tile_values)],
        injection,
        cotangent,
        node_mask.reshape(1, -1),
        spaces=[pltpu.SMEM] * 2 + [pltpu.HBM] * 3 + [pltpu.VMEM] * 3,
        scratch=[
            pltpu.SMEM(tile_rows.shape, jnp.int32),
            pltpu.SMEM(tile_cols.shape, jnp.int32),
            pltpu.VMEM((slots, TILE, TILE), BF16),
            pltpu.VMEM((n_y * n_col * 2 * LINE, TILE, TILE), F32),
            pltpu.SemaphoreType.DMA((2,)),
            pltpu.SemaphoreType.DMA((n_chunks,)),
        ],
    )

    def first_partial(near, far, *refs):
        a, outs = refs[:n_y], refs[n_y:]
        total = jnp.zeros((n_col * TILE, hidden), F32)
        for y in range(n_y):
            rows = slice(y * line_rows, (y + 1) * line_rows)
            total += jnp.dot(a[y][:, :line_rows], near[rows], preferred_element_type=F32)
            total += jnp.dot(a[y][:, line_rows : 2 * line_rows], far[rows], preferred_element_type=F32)
        outs[0][...] = total[:TILE]
        for x in range(1, n_col):
            outs[x][...] = total[x * TILE : (x + 1) * TILE].astype(BF16)

    n_square = len(square)
    square_rows = n_square * TILE

    def forward_near(z0, z1, z2, z3, *refs):
        a, out = refs[:n_y], refs[n_y]
        near = jnp.concatenate([z0[...], z1[...], z2[...], z3[...]], axis=0)
        rows = n_col * TILE
        for y in range(n_y):
            out[y * rows : (y + 1) * rows] = jnp.dot(a[y][:, :line_rows], near, preferred_element_type=F32)

    def far_product(held, far, a, y):
        rows = slice(y * n_col * TILE, (y + 1) * n_col * TILE)
        return held[rows] + jnp.dot(a[y][:, line_rows : 2 * line_rows], far[...], preferred_element_type=F32)

    def forward_far(held, far, *refs):
        a, outs = refs[:n_y], refs[n_y:]
        for y in range(n_y):
            total = far_product(held, far, a, y)
            for x in range(n_col):
                out = outs[y * n_col + x]
                out[...] = total[x * TILE : (x + 1) * TILE].astype(out.dtype)

    def forward_far_all(held, far, *refs):
        a, (kept, sent) = refs[:n_y], refs[n_y:]
        for y in range(n_y):
            rows = slice(y * n_col * TILE, (y + 1) * n_col * TILE)
            total = far_product(held, far, a, y)
            kept[rows] = total
            sent[rows] = total.astype(BF16)

    def advance(beta, peers):
        def body(*refs):
            sums, (w, anchor_ref, inject, out) = refs[:peers], refs[peers:]
            u = tree_sum([s[...].astype(F32) for s in sums])
            bent = jnp.tanh(split_dot(u, w[...], ((1,), (0,))) + inject[...].astype(F32))
            out[...] = (beta * anchor_ref[...].astype(F32) + (1.0 - beta) * bent).astype(BF16)

        return body

    def meet(kept, *refs):
        got, refs = refs[: n_square - 1], refs[n_square - 1 :]
        fixed_refs, (w, bent_out, slope_out, u_out, h_out) = refs[:n_col], refs[n_col:]
        fixed = [fixed_refs[x].at[2 * y * TILE : 2 * (y + 1) * TILE] for y, x in square]
        u = jnp.concatenate(
            [
                tree_sum(
                    [kept[j * TILE : (j + 1) * TILE]]
                    + [
                        got[i - 1][(i ^ j) * TILE : ((i ^ j) + 1) * TILE].astype(F32)
                        for i in range(1, n_square)
                    ]
                )
                for j in range(n_square)
            ],
            axis=0,
        )
        inject = jnp.concatenate([f[:TILE] for f in fixed], axis=0).astype(F32)
        bent = jnp.tanh(split_dot(u, w[...], ((1,), (0,))) + inject)
        slope = 1.0 - bent * bent
        base = jnp.concatenate([f[TILE:] for f in fixed], axis=0).astype(F32)
        h_out[...] = (base * slope).astype(BF16)
        bent_out[...] = bent[:TILE]
        slope_out[...] = slope[:TILE]
        u_out[...] = u[:TILE]

    def turn(fixed_ref, *refs):
        came, outs, fixed_out = refs[: n_y - 1], refs[n_y - 1 : -1], refs[-1]
        fixed_out[: 2 * TILE] = fixed_ref[...]
        for y in range(1, n_y):
            part, out = came[y - 1], outs[y - 1]
            fixed_out[2 * y * TILE : 2 * (y + 1) * TILE] = part[: 2 * TILE, 2 * line_rows :]
            for x in range(n_col):
                for p in range(2 * LINE):
                    here, there = slice(x * TILE, (x + 1) * TILE), slice(p * TILE, (p + 1) * TILE)
                    out[there, here] = part[here, there].T

    state = anchor
    for step in range(ITERS):
        beta = 1.0 / (step + 2.0)
        if step == 2:
            state, fixed_y = lax.optimization_barrier((state, fixed_y))
        line = [state] + along_line([state] * (LINE - 1))
        if step == 2:
            fixed = [fixed_y] + [exchange(fixed_y, 0, x) for x in range(1, n_col)]
            line, fixed = lax.optimization_barrier((line, fixed))
        if step == 0:
            joined = jnp.concatenate(line, axis=0)
            joined, *parts, turned = lax.optimization_barrier((joined, *parts, turned))
            bit = 2
            while bit < z_step:
                joined = jnp.concatenate([joined, exchange(joined, bit)], axis=0)
                bit *= 2
            joined, sent = lax.optimization_barrier((joined, parts[1:]))
            far = exchange(joined, 1)
            outs = [(block, F32)] + [(block, BF16)] * (n_col - 1)
            mine, *sends = vmem_call(first_partial, outs, joined, far, *parts)
            parts = [parts[0]] + [exchange(p, 2 * (i + 1)) for i, p in enumerate(sent)]
            got = [exchange(v, 0, x + 1) for x, v in enumerate(sends)]
        else:
            far = exchange(jnp.concatenate(line, axis=0), 1)
            (held,) = vmem_call(forward_near, [((square_rows, hidden), F32)], *line, *parts)
            if step == ITERS - 1:
                outs = [((square_rows, hidden), F32), ((square_rows, hidden), BF16)]
                kept, sent = vmem_call(forward_far_all, outs, held, far, *parts)
                got = to_square([sent] * (n_square - 1))
                bent, slope, mixed, h_all = vmem_call(
                    meet, [(block, F32)] * 3 + [((square_rows, hidden), BF16)], kept, *got, *fixed, weight
                )
                break
            outs = [(block, F32)] + [(block, BF16)] * (n_square - 1)
            mine, *sends = vmem_call(forward_far, outs, held, far, *parts)
            got = to_square(sends)
        if step == 1:
            *more, fixed_y = vmem_call(
                turn,
                [(part_shape[::-1], BF16)] * (n_y - 1) + [((2 * n_y * TILE, hidden), BF16)],
                fixed,
                *parts[1:],
            )
            turned = [turned] + more
        (state,) = vmem_call(
            advance(beta, 1 + len(got)), [(block, BF16)], mine, *got, weight, anchor, injection
        )

    def finish(bent_ref, anchor_ref, out):
        out[...] = (beta * anchor_ref[...].astype(F32) + (1.0 - beta) * bent_ref[...]).astype(BF16)

    (state,) = vmem_call(finish, [(block, BF16)], bent, anchor)

    def line_product(h, a_t, rows):
        total = None
        for y in range(n_y):
            if len(h) == 1:
                joined = h[0][y * n_col * TILE : (y + 1) * n_col * TILE]
            else:
                joined = jnp.concatenate([h[y * n_col + x][:TILE] for x in range(n_col)], axis=0)
            product = jnp.dot(a_t[y][rows], joined, preferred_element_type=F32)
            total = product if total is None else total + product
        return total

    def backward_near(n):
        def body(*refs):
            refs[-1][...] = line_product(refs[:n], refs[n:-1], slice(0, line_rows))

        return body

    def backward_far(n, last):
        def body(*refs):
            h, a_t, (far, *term) = refs[:n], refs[n : n + n_y], refs[n + n_y :]
            far[:line_rows] = line_product(h, a_t, slice(line_rows, 2 * line_rows)).astype(BF16)
            if last:
                whole = tree_sum([v[TILE:].astype(F32) for v in h])
                high, low = halves(whole)
                far[line_rows : line_rows + hidden] = high
                far[line_rows + hidden :] = low
                term[0][...] = high.astype(F32) + low.astype(F32)

        return body

    def fold(last):
        def body(held, got, *refs):
            outs = refs[1:] if last else refs
            for z in range(LINE):
                rows = slice(z * TILE, (z + 1) * TILE)
                value = held[rows] + got[rows].astype(F32)
                if z == 0:
                    outs[0][...] = value
                else:
                    outs[z][:TILE] = value.astype(BF16)
            if last:
                high, low = got[line_rows : line_rows + hidden], got[line_rows + hidden :]
                term = (refs[0][...] + (high.astype(F32) + low.astype(F32))).astype(BF16)
                outs[LINE][...] = term.astype(F32)
                for z in range(1, LINE):
                    outs[z][TILE:] = term

        return body

    def pull(last, ride):
        def body(held, *refs):
            got, rest = refs[: LINE - 1], refs[LINE - 1 :]
            v = tree_sum([held[...]] + [r[:TILE].astype(F32) for r in got])
            base, w, slope_ref = rest[:3]
            g = base[TILE : 2 * TILE].astype(F32) + split_dot(v, w[...], ((1,), (1,)))
            if last:
                term, adjoint_out, grad_out = rest[3:]
                adjoint_out[...] = g
                whole = tree_sum([term[...]] + [r[TILE:].astype(F32) for r in got])
                grad_out[...] = whole / (own * n_col)
            else:
                out = rest[-1]
                h = (g * slope_ref[...]).astype(BF16)
                out[:TILE] = h
                if ride:
                    out[TILE:] = split_dot(rest[3][...], h, ((0,), (0,))).astype(BF16)

        return body

    for step in range(ADJOINT):
        last, ride = step == ADJOINT - 1, step == ADJOINT - 2
        states = [h_all] if step == 0 else [scaled] + to_square([scaled] * (n_square - 1))
        extra = 2 * hidden if last else 0
        far, *term = vmem_call(
            backward_far(len(states), last),
            [((line_rows + extra, hidden), BF16)] + ([((hidden, hidden), F32)] if last else []),
            *states,
            *turned,
        )
        (near,) = vmem_call(
            backward_near(len(states)), [((line_rows, hidden), F32)], *states, *turned
        )
        got = exchange(far, 1)
        extra = hidden if last else 0
        held, *sends = vmem_call(
            fold(last),
            [(block, F32)]
            + [((TILE + extra, hidden), BF16)] * (LINE - 1)
            + ([((hidden, hidden), F32)] if last else []),
            near,
            got,
            *term,
        )
        if last:
            *sends, total = sends
        got = along_line(sends)
        inputs = (held, *got, fixed[0], weight, slope)
        if last:
            adjoint, weight_grad = vmem_call(
                pull(True, False), [(block, F32), ((hidden, hidden), F32)], *inputs, total
            )
        else:
            rows = TILE + (hidden if ride else 0)
            (scaled,) = vmem_call(
                pull(False, ride), [((rows, hidden), BF16)], *inputs, *([mixed] if ride else [])
            )
    return state, adjoint, weight_grad


def solution(mesh):
    in_specs = (
        P(("row", "col"), None),
        P(("row", "col"), None),
        P(),
        P(("row", "col"), None),
        P(("row", "col")),
        P("row", "col", None, None, None),
        P("row", "col", None),
        P("row", "col", None),
        P("row", "col"),
    )
    out_specs = (P(("row", "col"), None), P(("row", "col"), None), P())

    def whole(*args):
        return per_device(mesh.shape["row"], mesh.shape["col"], *args)

    return jax.shard_map(whole, mesh=mesh, in_specs=in_specs, out_specs=out_specs, check_vma=False)
```

```python
import jax
import jax.numpy as jnp
from jax import lax
from jax.experimental import pallas as pl
from jax.experimental.pallas import tpu as pltpu
from jax.sharding import PartitionSpec as P

TILE = 128
ITERS = 3
ADJOINT = 3
LINE = 4
BF16 = jnp.bfloat16
F32 = jnp.float32
VMEM_LIMIT = 48 * 2**20


def vmem_call(body, outs, *args, spaces=None, scratch=()):
    specs = [pl.BlockSpec(memory_space=space) for space in spaces or [pltpu.VMEM] * len(args)]
    out_specs = [pl.BlockSpec(memory_space=pltpu.VMEM) for _ in outs]
    return pl.pallas_call(
        body,
        out_shape=[jax.ShapeDtypeStruct(shape, dtype) for shape, dtype in outs],
        in_specs=specs,
        out_specs=out_specs,
        scratch_shapes=list(scratch),
        compiler_params=pltpu.CompilerParams(vmem_limit_bytes=VMEM_LIMIT),
    )(*args)


def halves(value):
    high = value.astype(BF16)
    return high, (value - high.astype(F32)).astype(BF16)


def split_dot(value, factor, dims):
    high, low = halves(value)
    return lax.dot_general(high, factor, (dims, ((), ())), preferred_element_type=F32) + lax.dot_general(
        low, factor, (dims, ((), ())), preferred_element_type=F32
    )


def tree_sum(values):
    while len(values) > 1:
        values = [values[i] + values[i + 1] for i in range(0, len(values), 2)]
    return values[0]


def per_device(n_row, n_col, *args):
    anchor, injection, weight, cotangent, node_mask, tile_values, tile_rows, tile_cols, tile_counts = args
    own, hidden = anchor.shape
    assert own == TILE
    slots = tile_values.shape[2]
    z_step = n_row // LINE
    n_y = z_step // 2
    square = [(y, x) for y in range(n_y) for x in range(n_col)]
    line_rows = LINE * TILE
    block = (TILE, hidden)
    where = jnp.stack([lax.axis_index("row"), lax.axis_index("col")]).astype(jnp.int32)

    def exchange(value, row_xor, col_xor=0):
        if col_xor == 0:
            return lax.ppermute(value, "row", [(i, i ^ row_xor) for i in range(n_row)])
        if row_xor == 0:
            return lax.ppermute(value, "col", [(i, i ^ col_xor) for i in range(n_col)])
        pairs = [
            (r * n_col + c, (r ^ row_xor) * n_col + (c ^ col_xor))
            for r in range(n_row)
            for c in range(n_col)
        ]
        return lax.ppermute(value, ("row", "col"), pairs)

    def along_line(values):
        return [exchange(v, z * z_step) for z, v in zip(range(1, LINE), values)]

    def to_square(values):
        return [exchange(v, 2 * y, x) for (y, x), v in zip(square[1:], values)]

    chunk = min(16, slots)
    n_chunks = slots // chunk
    assert slots % chunk == 0

    def build(where_ref, count, *refs):
        small_hbm, tiles_hbm, refs = refs[:5], refs[5], refs[6:]
        parts, turned, fixed_out = refs[:n_y], refs[n_y], refs[n_y + 1]
        small, (tiles, acc, small_sem, tile_sem) = refs[n_y + 2 : n_y + 7], refs[n_y + 7 :]
        rows, cols, inject, cotan, mask = small
        copies = [
            pltpu.make_async_copy(source, target, small_sem.at[i])
            for i, (source, target) in enumerate(zip(small_hbm, small))
        ]
        pieces = [slice(c * chunk, (c + 1) * chunk) for c in range(n_chunks)]
        loads = [
            pltpu.make_async_copy(tiles_hbm.at[0, 0, piece], tiles.at[piece], tile_sem.at[c])
            for c, piece in enumerate(pieces)
        ]
        for copy in copies + loads:
            copy.start()
        acc[...] = jnp.zeros_like(acc)
        for copy in copies:
            copy.wait()
        fixed_out[:TILE] = inject[...]
        kept_nodes = jnp.broadcast_to(mask[...].astype(F32), (TILE, TILE)).T[:, :1]
        fixed_out[TILE:] = (cotan[...].astype(F32) * kept_nodes).astype(BF16)

        def add(k, carry):
            s = cols[0, 0, k] ^ where_ref[0]
            x = rows[0, 0, k] ^ where_ref[1]
            y = (s // 2) % n_y
            acc[((y * n_col + x) * 2 + s % 2) * LINE + s // z_step] += tiles[k].astype(F32)
            return carry

        for c, load in enumerate(loads):
            load.wait()
            lax.fori_loop(c * chunk, jnp.clip(count[0, 0], c * chunk, (c + 1) * chunk), add, 0)
        for y in range(n_y):
            for x in range(n_col):
                for p in range(2 * LINE):
                    tile = acc[(y * n_col + x) * 2 * LINE + p]
                    here, there = slice(x * TILE, (x + 1) * TILE), slice(p * TILE, (p + 1) * TILE)
                    parts[y][here, there] = tile.astype(BF16)
                    if y == 0:
                        turned[there, here] = tile.T.astype(BF16)
            if y > 0:
                parts[y][: 2 * TILE, 2 * line_rows :] = fixed_out[...]
                if n_col > 2:
                    parts[y][2 * TILE :, 2 * line_rows :] = jnp.zeros(((n_col - 2) * TILE, hidden), BF16)

    assert n_col >= 2
    part_shape = (n_col * TILE, 2 * line_rows)
    sent_shape = (n_col * TILE, 2 * line_rows + hidden)
    small = (tile_rows, tile_cols, injection, cotangent, node_mask.reshape(1, -1))
    *parts, turned, fixed = vmem_call(
        build,
        [(part_shape, BF16)] + [(sent_shape, BF16)] * (n_y - 1)
        + [(part_shape[::-1], BF16), ((2 * TILE, hidden), BF16)],
        where,
        tile_counts,
        *[pltpu.with_memory_space_constraint(v, pltpu.HBM) for v in (*small, tile_values)],
        spaces=[pltpu.SMEM] * 2 + [pltpu.HBM] * 6,
        scratch=[
            *[pltpu.SMEM(v.shape, v.dtype) for v in small[:2]],
            *[pltpu.VMEM(v.shape, v.dtype) for v in small[2:]],
            pltpu.VMEM((slots, TILE, TILE), BF16),
            pltpu.VMEM((n_y * n_col * 2 * LINE, TILE, TILE), F32),
            pltpu.SemaphoreType.DMA((5,)),
            pltpu.SemaphoreType.DMA((n_chunks,)),
        ],
    )

    def first_partial(near, far, *refs):
        a, outs = refs[:n_y], refs[n_y:]
        total = jnp.zeros((n_col * TILE, hidden), F32)
        for y in range(n_y):
            rows = slice(y * line_rows, (y + 1) * line_rows)
            total += jnp.dot(a[y][:, :line_rows], near[rows], preferred_element_type=F32)
            total += jnp.dot(a[y][:, line_rows : 2 * line_rows], far[rows], preferred_element_type=F32)
        outs[0][...] = total[:TILE]
        for x in range(1, n_col):
            outs[x][...] = total[x * TILE : (x + 1) * TILE].astype(BF16)

    n_square = len(square)
    square_rows = n_square * TILE

    def forward_near(z0, z1, z2, z3, *refs):
        a, out = refs[:n_y], refs[n_y]
        near = jnp.concatenate([z0[...], z1[...], z2[...], z3[...]], axis=0)
        rows = n_col * TILE
        for y in range(n_y):
            out[y * rows : (y + 1) * rows] = jnp.dot(a[y][:, :line_rows], near, preferred_element_type=F32)

    def far_product(held, far, a, y):
        rows = slice(y * n_col * TILE, (y + 1) * n_col * TILE)
        return held[rows] + jnp.dot(a[y][:, line_rows : 2 * line_rows], far[...], preferred_element_type=F32)

    def forward_far(held, far, *refs):
        a, outs = refs[:n_y], refs[n_y:]
        for y in range(n_y):
            total = far_product(held, far, a, y)
            for x in range(n_col):
                out = outs[y * n_col + x]
                out[...] = total[x * TILE : (x + 1) * TILE].astype(out.dtype)

    def forward_far_all(held, far, *refs):
        a, (kept, sent) = refs[:n_y], refs[n_y:]
        for y in range(n_y):
            rows = slice(y * n_col * TILE, (y + 1) * n_col * TILE)
            total = far_product(held, far, a, y)
            kept[rows] = total
            sent[rows] = total.astype(BF16)

    def advance(beta, peers):
        def body(*refs):
            sums, (w, anchor_ref, inject, out) = refs[:peers], refs[peers:]
            u = tree_sum([s[...].astype(F32) for s in sums])
            bent = jnp.tanh(split_dot(u, w[...], ((1,), (0,))) + inject[...].astype(F32))
            out[...] = (beta * anchor_ref[...].astype(F32) + (1.0 - beta) * bent).astype(BF16)

        return body

    def meet(kept, *refs):
        got, refs = refs[: n_square - 1], refs[n_square - 1 :]
        fixed_refs, (w, bent_out, slope_out, u_out, h_out) = refs[:n_col], refs[n_col:]
        fixed = [fixed_refs[x].at[2 * y * TILE : 2 * (y + 1) * TILE] for y, x in square]
        u = jnp.concatenate(
            [
                tree_sum(
                    [kept[j * TILE : (j + 1) * TILE]]
                    + [
                        got[i - 1][(i ^ j) * TILE : ((i ^ j) + 1) * TILE].astype(F32)
                        for i in range(1, n_square)
                    ]
                )
                for j in range(n_square)
            ],
            axis=0,
        )
        inject = jnp.concatenate([f[:TILE] for f in fixed], axis=0).astype(F32)
        bent = jnp.tanh(split_dot(u, w[...], ((1,), (0,))) + inject)
        slope = 1.0 - bent * bent
        base = jnp.concatenate([f[TILE:] for f in fixed], axis=0).astype(F32)
        h_out[...] = (base * slope).astype(BF16)
        bent_out[...] = bent[:TILE]
        slope_out[...] = slope[:TILE]
        u_out[...] = u[:TILE]

    def turn(fixed_ref, *refs):
        came, outs, fixed_out = refs[: n_y - 1], refs[n_y - 1 : -1], refs[-1]
        fixed_out[: 2 * TILE] = fixed_ref[...]
        for y in range(1, n_y):
            part, out = came[y - 1], outs[y - 1]
            fixed_out[2 * y * TILE : 2 * (y + 1) * TILE] = part[: 2 * TILE, 2 * line_rows :]
            for x in range(n_col):
                for p in range(2 * LINE):
                    here, there = slice(x * TILE, (x + 1) * TILE), slice(p * TILE, (p + 1) * TILE)
                    out[there, here] = part[here, there].T

    state = anchor
    for step in range(ITERS):
        beta = 1.0 / (step + 2.0)
        if step == 2:
            state, fixed_y = lax.optimization_barrier((state, fixed_y))
        line = [state] + along_line([state] * (LINE - 1))
        if step == 2:
            fixed = [fixed_y] + [exchange(fixed_y, 0, x) for x in range(1, n_col)]
            line, fixed = lax.optimization_barrier((line, fixed))
        if step == 0:
            joined = jnp.concatenate(line, axis=0)
            joined, *parts, turned = lax.optimization_barrier((joined, *parts, turned))
            bit = 2
            while bit < z_step:
                joined = jnp.concatenate([joined, exchange(joined, bit)], axis=0)
                bit *= 2
            sent = parts[1:]
            far = exchange(joined, 1)
            outs = [(block, F32)] + [(block, BF16)] * (n_col - 1)
            mine, *sends = vmem_call(first_partial, outs, joined, far, *parts)
            parts = [parts[0]] + [exchange(p, 2 * (i + 1)) for i, p in enumerate(sent)]
            got = [exchange(v, 0, x + 1) for x, v in enumerate(sends)]
        else:
            far = exchange(jnp.concatenate(line, axis=0), 1)
            (held,) = vmem_call(forward_near, [((square_rows, hidden), F32)], *line, *parts)
            if step == ITERS - 1:
                outs = [((square_rows, hidden), F32), ((square_rows, hidden), BF16)]
                kept, sent = vmem_call(forward_far_all, outs, held, far, *parts)
                got = to_square([sent] * (n_square - 1))
                bent, slope, mixed, h_all = vmem_call(
                    meet, [(block, F32)] * 3 + [((square_rows, hidden), BF16)], kept, *got, *fixed, weight
                )
                break
            outs = [(block, F32)] + [(block, BF16)] * (n_square - 1)
            mine, *sends = vmem_call(forward_far, outs, held, far, *parts)
            got = to_square(sends)
        if step == 1:
            *more, fixed_y = vmem_call(
                turn,
                [(part_shape[::-1], BF16)] * (n_y - 1) + [((2 * n_y * TILE, hidden), BF16)],
                fixed,
                *parts[1:],
            )
            turned = [turned] + more
        (state,) = vmem_call(
            advance(beta, 1 + len(got)), [(block, BF16)], mine, *got, weight, anchor, injection
        )

    def finish(bent_ref, anchor_ref, out):
        out[...] = (beta * anchor_ref[...].astype(F32) + (1.0 - beta) * bent_ref[...]).astype(BF16)

    (state,) = vmem_call(finish, [(block, BF16)], bent, anchor)

    def line_product(h, a_t, rows):
        total = None
        for y in range(n_y):
            if len(h) == 1:
                joined = h[0][y * n_col * TILE : (y + 1) * n_col * TILE]
            else:
                joined = jnp.concatenate([h[y * n_col + x][:TILE] for x in range(n_col)], axis=0)
            product = jnp.dot(a_t[y][rows], joined, preferred_element_type=F32)
            total = product if total is None else total + product
        return total

    def backward_near(n):
        def body(*refs):
            refs[-1][...] = line_product(refs[:n], refs[n:-1], slice(0, line_rows))

        return body

    def backward_far(n, last):
        def body(*refs):
            h, a_t, (far, *term) = refs[:n], refs[n : n + n_y], refs[n + n_y :]
            far[:line_rows] = line_product(h, a_t, slice(line_rows, 2 * line_rows)).astype(BF16)
            if last:
                whole = tree_sum([v[TILE:].astype(F32) for v in h])
                high, low = halves(whole)
                far[line_rows : line_rows + hidden] = high
                far[line_rows + hidden :] = low
                term[0][...] = high.astype(F32) + low.astype(F32)

        return body

    def fold(last):
        def body(held, got, *refs):
            outs = refs[1:] if last else refs
            for z in range(LINE):
                rows = slice(z * TILE, (z + 1) * TILE)
                value = held[rows] + got[rows].astype(F32)
                if z == 0:
                    outs[0][...] = value
                else:
                    outs[z][:TILE] = value.astype(BF16)
            if last:
                high, low = got[line_rows : line_rows + hidden], got[line_rows + hidden :]
                term = (refs[0][...] + (high.astype(F32) + low.astype(F32))).astype(BF16)
                outs[LINE][...] = term.astype(F32)
                for z in range(1, LINE):
                    outs[z][TILE:] = term

        return body

    def pull(last, ride):
        def body(held, *refs):
            got, rest = refs[: LINE - 1], refs[LINE - 1 :]
            v = tree_sum([held[...]] + [r[:TILE].astype(F32) for r in got])
            base, w, slope_ref = rest[:3]
            g = base[TILE : 2 * TILE].astype(F32) + split_dot(v, w[...], ((1,), (1,)))
            if last:
                term, adjoint_out, grad_out = rest[3:]
                adjoint_out[...] = g
                whole = tree_sum([term[...]] + [r[TILE:].astype(F32) for r in got])
                grad_out[...] = whole / (own * n_col)
            else:
                out = rest[-1]
                h = (g * slope_ref[...]).astype(BF16)
                out[:TILE] = h
                if ride:
                    out[TILE:] = split_dot(rest[3][...], h, ((0,), (0,))).astype(BF16)

        return body

    for step in range(ADJOINT):
        last, ride = step == ADJOINT - 1, step == ADJOINT - 2
        states = [h_all] if step == 0 else [scaled] + to_square([scaled] * (n_square - 1))
        extra = 2 * hidden if last else 0
        far, *term = vmem_call(
            backward_far(len(states), last),
            [((line_rows + extra, hidden), BF16)] + ([((hidden, hidden), F32)] if last else []),
            *states,
            *turned,
        )
        (near,) = vmem_call(
            backward_near(len(states)), [((line_rows, hidden), F32)], *states, *turned
        )
        got = exchange(far, 1)
        extra = hidden if last else 0
        held, *sends = vmem_call(
            fold(last),
            [(block, F32)]
            + [((TILE + extra, hidden), BF16)] * (LINE - 1)
            + ([((hidden, hidden), F32)] if last else []),
            near,
            got,
            *term,
        )
        if last:
            *sends, total = sends
        got = along_line(sends)
        inputs = (held, *got, fixed[0], weight, slope)
        if last:
            adjoint, weight_grad = vmem_call(
                pull(True, False), [(block, F32), ((hidden, hidden), F32)], *inputs, total
            )
        else:
            rows = TILE + (hidden if ride else 0)
            (scaled,) = vmem_call(
                pull(False, ride), [((rows, hidden), BF16)], *inputs, *([mixed] if ride else [])
            )
    return state, adjoint, weight_grad


def solution(mesh):
    in_specs = (
        P(("row", "col"), None),
        P(("row", "col"), None),
        P(),
        P(("row", "col"), None),
        P(("row", "col")),
        P("row", "col", None, None, None),
        P("row", "col", None),
        P("row", "col", None),
        P("row", "col"),
    )
    out_specs = (P(("row", "col"), None), P(("row", "col"), None), P())

    def whole(*args):
        return per_device(mesh.shape["row"], mesh.shape["col"], *args)

    return jax.shard_map(whole, mesh=mesh, in_specs=in_specs, out_specs=out_specs, check_vma=False)
```

```python
import jax
import jax.numpy as jnp
from jax import lax
from jax.experimental import pallas as pl
from jax.experimental.pallas import tpu as pltpu
from jax.sharding import PartitionSpec as P

TILE = 128
ITERS = 3
ADJOINT = 3
LINE = 4
BF16 = jnp.bfloat16
F32 = jnp.float32
VMEM_LIMIT = 48 * 2**20


def vmem_call(body, outs, *args, spaces=None, scratch=()):
    specs = [pl.BlockSpec(memory_space=space) for space in spaces or [pltpu.VMEM] * len(args)]
    out_specs = [pl.BlockSpec(memory_space=pltpu.VMEM) for _ in outs]
    return pl.pallas_call(
        body,
        out_shape=[jax.ShapeDtypeStruct(shape, dtype) for shape, dtype in outs],
        in_specs=specs,
        out_specs=out_specs,
        scratch_shapes=list(scratch),
        compiler_params=pltpu.CompilerParams(vmem_limit_bytes=VMEM_LIMIT),
    )(*args)


def halves(value):
    high = value.astype(BF16)
    return high, (value - high.astype(F32)).astype(BF16)


def split_dot(value, factor, dims):
    high, low = halves(value)
    return lax.dot_general(high, factor, (dims, ((), ())), preferred_element_type=F32) + lax.dot_general(
        low, factor, (dims, ((), ())), preferred_element_type=F32
    )


def tree_sum(values):
    while len(values) > 1:
        values = [values[i] + values[i + 1] for i in range(0, len(values), 2)]
    return values[0]


def per_device(n_row, n_col, *args):
    anchor, injection, weight, cotangent, node_mask, tile_values, tile_rows, tile_cols, tile_counts = args
    own, hidden = anchor.shape
    assert own == TILE
    slots = tile_values.shape[2]
    z_step = n_row // LINE
    n_y = z_step // 2
    square = [(y, x) for y in range(n_y) for x in range(n_col)]
    line_rows = LINE * TILE
    block = (TILE, hidden)
    where = jnp.stack([lax.axis_index("row"), lax.axis_index("col")]).astype(jnp.int32)

    def exchange(value, row_xor, col_xor=0):
        if col_xor == 0:
            return lax.ppermute(value, "row", [(i, i ^ row_xor) for i in range(n_row)])
        if row_xor == 0:
            return lax.ppermute(value, "col", [(i, i ^ col_xor) for i in range(n_col)])
        pairs = [
            (r * n_col + c, (r ^ row_xor) * n_col + (c ^ col_xor))
            for r in range(n_row)
            for c in range(n_col)
        ]
        return lax.ppermute(value, ("row", "col"), pairs)

    def along_line(values):
        return [exchange(v, z * z_step) for z, v in zip(range(1, LINE), values)]

    def to_square(values):
        return [exchange(v, 2 * y, x) for (y, x), v in zip(square[1:], values)]

    chunk = min(16, slots)
    n_chunks = slots // chunk
    assert slots % chunk == 0

    def build(where_ref, count, *refs):
        small_hbm, tiles_hbm, refs = refs[:5], refs[5], refs[6:]
        parts, turned, fixed_out = refs[:n_y], refs[n_y], refs[n_y + 1]
        small, (tiles, acc, small_sem, tile_sem) = refs[n_y + 2 : n_y + 7], refs[n_y + 7 :]
        rows, cols, inject, cotan, mask = small
        copies = [
            pltpu.make_async_copy(source, target, small_sem.at[i])
            for i, (source, target) in enumerate(zip(small_hbm, small))
        ]
        pieces = [slice(c * chunk, (c + 1) * chunk) for c in range(n_chunks)]
        loads = [
            pltpu.make_async_copy(tiles_hbm.at[0, 0, piece], tiles.at[piece], tile_sem.at[c])
            for c, piece in enumerate(pieces)
        ]
        for copy in copies + loads:
            copy.start()
        acc[...] = jnp.zeros_like(acc)
        for copy in copies:
            copy.wait()
        fixed_out[:TILE] = inject[...]
        kept_nodes = jnp.broadcast_to(mask[...].astype(F32), (TILE, TILE)).T[:, :1]
        fixed_out[TILE:] = (cotan[...].astype(F32) * kept_nodes).astype(BF16)

        def add(k, carry):
            s = cols[0, 0, k] ^ where_ref[0]
            x = rows[0, 0, k] ^ where_ref[1]
            y = (s // 2) % n_y
            acc[((y * n_col + x) * 2 + s % 2) * LINE + s // z_step] += tiles[k].astype(F32)
            return carry

        for c, load in enumerate(loads):
            load.wait()
            lax.fori_loop(c * chunk, jnp.clip(count[0, 0], c * chunk, (c + 1) * chunk), add, 0)
        for y in range(n_y):
            for x in range(n_col):
                for p in range(2 * LINE):
                    tile = acc[(y * n_col + x) * 2 * LINE + p]
                    here, there = slice(x * TILE, (x + 1) * TILE), slice(p * TILE, (p + 1) * TILE)
                    parts[y][here, there] = tile.astype(BF16)
                    if y == 0:
                        turned[there, here] = tile.T.astype(BF16)
            if y > 0:
                parts[y][: 2 * TILE, 2 * line_rows :] = fixed_out[...]
                if n_col > 2:
                    parts[y][2 * TILE :, 2 * line_rows :] = jnp.zeros(((n_col - 2) * TILE, hidden), BF16)

    assert n_col >= 2
    part_shape = (n_col * TILE, 2 * line_rows)
    sent_shape = (n_col * TILE, 2 * line_rows + hidden)
    small = (tile_rows, tile_cols, injection, cotangent, node_mask.reshape(1, -1))
    *parts, turned, fixed = vmem_call(
        build,
        [(part_shape, BF16)] + [(sent_shape, BF16)] * (n_y - 1)
        + [(part_shape[::-1], BF16), ((2 * TILE, hidden), BF16)],
        where,
        tile_counts,
        *[pltpu.with_memory_space_constraint(v, pltpu.HBM) for v in (*small, tile_values)],
        spaces=[pltpu.SMEM] * 2 + [pltpu.HBM] * 6,
        scratch=[
            *[pltpu.SMEM(v.shape, v.dtype) for v in small[:2]],
            *[pltpu.VMEM(v.shape, v.dtype) for v in small[2:]],
            pltpu.VMEM((slots, TILE, TILE), BF16),
            pltpu.VMEM((n_y * n_col * 2 * LINE, TILE, TILE), F32),
            pltpu.SemaphoreType.DMA((5,)),
            pltpu.SemaphoreType.DMA((n_chunks,)),
        ],
    )

    def own_product(block_rows, a, side):
        total = None
        for y in range(n_y):
            part = a[y][:, side * line_rows : (side + 1) * line_rows]
            rows = block_rows[y * line_rows : (y + 1) * line_rows]
            product = jnp.dot(part, rows, preferred_element_type=F32)
            total = product if total is None else total + product
        return total

    def first_near(near, *refs):
        refs[n_y][...] = own_product(near, refs[:n_y], 0)

    def first_far(held, far, *refs):
        a, outs = refs[:n_y], refs[n_y:]
        total = held[...] + own_product(far, a, 1)
        for x in range(n_col):
            outs[x][...] = total[x * TILE : (x + 1) * TILE].astype(outs[x].dtype)

    n_square = len(square)
    square_rows = n_square * TILE

    def forward_near(z0, z1, z2, z3, *refs):
        a, out = refs[:n_y], refs[n_y]
        near = jnp.concatenate([z0[...], z1[...], z2[...], z3[...]], axis=0)
        rows = n_col * TILE
        for y in range(n_y):
            out[y * rows : (y + 1) * rows] = jnp.dot(a[y][:, :line_rows], near, preferred_element_type=F32)

    def far_product(held, far, a, y):
        rows = slice(y * n_col * TILE, (y + 1) * n_col * TILE)
        return held[rows] + jnp.dot(a[y][:, line_rows : 2 * line_rows], far[...], preferred_element_type=F32)

    def forward_far(held, far, fixed_ref, *refs):
        a, outs = refs[:n_y], refs[n_y:]
        for y in range(n_y):
            total = far_product(held, far, a, y)
            for x in range(n_col):
                out = outs[y * n_col + x]
                out[:TILE] = total[x * TILE : (x + 1) * TILE].astype(out.dtype)
                if x > 0:
                    out[TILE:] = fixed_ref[...]

    def forward_far_all(held, far, *refs):
        a, (kept, sent) = refs[:n_y], refs[n_y:]
        for y in range(n_y):
            rows = slice(y * n_col * TILE, (y + 1) * n_col * TILE)
            total = far_product(held, far, a, y)
            kept[rows] = total
            sent[rows] = total.astype(BF16)

    def advance(beta, peers):
        def body(*refs):
            sums, (w, anchor_ref, inject, out) = refs[:peers], refs[peers:]
            u = tree_sum([s[:TILE].astype(F32) for s in sums])
            bent = jnp.tanh(split_dot(u, w[...], ((1,), (0,))) + inject[...].astype(F32))
            out[...] = (beta * anchor_ref[...].astype(F32) + (1.0 - beta) * bent).astype(BF16)

        return body

    def meet(kept, *refs):
        got, refs = refs[: n_square - 1], refs[n_square - 1 :]
        by_y, by_x, (w, bent_out, slope_out, u_out, h_out) = refs[0], refs[1 : -5], refs[-5:]
        by_x = iter(by_x)
        fixed = [
            by_y.at[2 * y * TILE : 2 * (y + 1) * TILE] if x == 0 else next(by_x).at[TILE : 3 * TILE]
            for y, x in square
        ]
        u = jnp.concatenate(
            [
                tree_sum(
                    [kept[j * TILE : (j + 1) * TILE]]
                    + [
                        got[i - 1][(i ^ j) * TILE : ((i ^ j) + 1) * TILE].astype(F32)
                        for i in range(1, n_square)
                    ]
                )
                for j in range(n_square)
            ],
            axis=0,
        )
        inject = jnp.concatenate([f[:TILE] for f in fixed], axis=0).astype(F32)
        bent = jnp.tanh(split_dot(u, w[...], ((1,), (0,))) + inject)
        slope = 1.0 - bent * bent
        base = jnp.concatenate([f[TILE:] for f in fixed], axis=0).astype(F32)
        h_out[...] = (base * slope).astype(BF16)
        bent_out[...] = bent[:TILE]
        slope_out[...] = slope[:TILE]
        u_out[...] = u[:TILE]

    def turn(fixed_ref, *refs):
        came, outs, fixed_out = refs[: n_y - 1], refs[n_y - 1 : -1], refs[-1]
        fixed_out[: 2 * TILE] = fixed_ref[...]
        for y in range(1, n_y):
            part, out = came[y - 1], outs[y - 1]
            fixed_out[2 * y * TILE : 2 * (y + 1) * TILE] = part[: 2 * TILE, 2 * line_rows :]
            for x in range(n_col):
                for p in range(2 * LINE):
                    here, there = slice(x * TILE, (x + 1) * TILE), slice(p * TILE, (p + 1) * TILE)
                    out[there, here] = part[here, there].T

    state = anchor
    for step in range(ITERS):
        beta = 1.0 / (step + 2.0)
        line = [state] + along_line([state] * (LINE - 1))
        if step == 0:
            joined = jnp.concatenate(line, axis=0)
            joined, *parts, turned = lax.optimization_barrier((joined, *parts, turned))
            bit = 2
            while bit < z_step:
                joined = jnp.concatenate([joined, exchange(joined, bit)], axis=0)
                bit *= 2
            sent = parts[1:]
            far = exchange(joined, 1)
            (held,) = vmem_call(first_near, [((n_col * TILE, hidden), F32)], joined, *parts)
            outs = [(block, F32)] + [(block, BF16)] * (n_col - 1)
            mine, *sends = vmem_call(first_far, outs, held, far, *parts)
            parts = [parts[0]] + [exchange(p, 2 * (i + 1)) for i, p in enumerate(sent)]
            got = [exchange(v, 0, x + 1) for x, v in enumerate(sends)]
        else:
            far = exchange(jnp.concatenate(line, axis=0), 1)
            (held,) = vmem_call(forward_near, [((square_rows, hidden), F32)], *line, *parts)
            if step == ITERS - 1:
                outs = [((square_rows, hidden), F32), ((square_rows, hidden), BF16)]
                kept, sent = vmem_call(forward_far_all, outs, held, far, *parts)
                got = to_square([sent] * (n_square - 1))
                bent, slope, mixed, h_all = vmem_call(
                    meet, [(block, F32)] * 3 + [((square_rows, hidden), BF16)], kept, *got, fixed_y, *fixed_x, weight
                )
                break
            outs = [(block, F32)] + [((TILE if x == 0 else 3 * TILE, hidden), BF16) for y, x in square[1:]]
            mine, *sends = vmem_call(forward_far, outs, held, far, fixed, *parts)
            got = to_square(sends)
            fixed_x = [v for (y, x), v in zip(square[1:], got) if x > 0]
        if step == 1:
            *more, fixed_y = vmem_call(
                turn,
                [(part_shape[::-1], BF16)] * (n_y - 1) + [((2 * n_y * TILE, hidden), BF16)],
                fixed,
                *parts[1:],
            )
            turned = [turned] + more
        (state,) = vmem_call(
            advance(beta, 1 + len(got)), [(block, BF16)], mine, *got, weight, anchor, injection
        )

    def finish(bent_ref, anchor_ref, u, out, high, low):
        out[...] = (beta * anchor_ref[...].astype(F32) + (1.0 - beta) * bent_ref[...]).astype(BF16)
        high[...], low[...] = halves(u[...].T)

    state, *mixed = vmem_call(
        finish, [(block, BF16)] + [((hidden, TILE), BF16)] * 2, bent, anchor, mixed
    )

    def line_product(h, a_t, rows):
        total = None
        for y in range(n_y):
            if len(h) == 1:
                joined = h[0][y * n_col * TILE : (y + 1) * n_col * TILE]
            else:
                joined = jnp.concatenate([h[y * n_col + x][:TILE] for x in range(n_col)], axis=0)
            product = jnp.dot(a_t[y][rows], joined, preferred_element_type=F32)
            total = product if total is None else total + product
        return total

    def backward_near(n):
        def body(*refs):
            refs[-1][...] = line_product(refs[:n], refs[n:-1], slice(0, line_rows))

        return body

    def backward_far(n, last):
        def body(*refs):
            h, a_t, (far, *term) = refs[:n], refs[n : n + n_y], refs[n + n_y :]
            far[:line_rows] = line_product(h, a_t, slice(line_rows, 2 * line_rows)).astype(BF16)
            if last:
                whole = tree_sum([v[TILE:].astype(F32) for v in h])
                high, low = halves(whole)
                far[line_rows : line_rows + hidden] = high
                far[line_rows + hidden :] = low
                term[0][...] = high.astype(F32) + low.astype(F32)

        return body

    def fold(last):
        def body(held, got, *refs):
            outs = refs[1:] if last else refs
            for z in range(LINE):
                rows = slice(z * TILE, (z + 1) * TILE)
                value = held[rows] + got[rows].astype(F32)
                if z == 0:
                    outs[0][...] = value
                else:
                    outs[z][:TILE] = value.astype(BF16)
            if last:
                high, low = got[line_rows : line_rows + hidden], got[line_rows + hidden :]
                term = (refs[0][...] + (high.astype(F32) + low.astype(F32))).astype(BF16)
                outs[LINE][...] = term.astype(F32)
                for z in range(1, LINE):
                    outs[z][TILE:] = term

        return body

    def pull(last, ride):
        def body(held, *refs):
            got, rest = refs[: LINE - 1], refs[LINE - 1 :]
            v = tree_sum([held[...]] + [r[:TILE].astype(F32) for r in got])
            base, w, slope_ref = rest[:3]
            g = base[TILE : 2 * TILE].astype(F32) + split_dot(v, w[...], ((1,), (1,)))
            if last:
                term, adjoint_out, grad_out = rest[3:]
                adjoint_out[...] = g
                whole = tree_sum([term[...]] + [r[TILE:].astype(F32) for r in got])
                grad_out[...] = whole / (own * n_col)
            else:
                out = rest[-1]
                h = (g * slope_ref[...]).astype(BF16)
                out[:TILE] = h
                if ride:
                    term = jnp.dot(rest[3][...], h, preferred_element_type=F32)
                    term += jnp.dot(rest[4][...], h, preferred_element_type=F32)
                    out[TILE:] = term.astype(BF16)

        return body

    for step in range(ADJOINT):
        last, ride = step == ADJOINT - 1, step == ADJOINT - 2
        states = [h_all] if step == 0 else [scaled] + to_square([scaled] * (n_square - 1))
        extra = 2 * hidden if last else 0
        far, *term = vmem_call(
            backward_far(len(states), last),
            [((line_rows + extra, hidden), BF16)] + ([((hidden, hidden), F32)] if last else []),
            *states,
            *turned,
        )
        (near,) = vmem_call(
            backward_near(len(states)), [((line_rows, hidden), F32)], *states, *turned
        )
        got = exchange(far, 1)
        extra = hidden if last else 0
        held, *sends = vmem_call(
            fold(last),
            [(block, F32)]
            + [((TILE + extra, hidden), BF16)] * (LINE - 1)
            + ([((hidden, hidden), F32)] if last else []),
            near,
            got,
            *term,
        )
        if last:
            *sends, total = sends
        got = along_line(sends)
        inputs = (held, *got, fixed, weight, slope)
        if last:
            adjoint, weight_grad = vmem_call(
                pull(True, False), [(block, F32), ((hidden, hidden), F32)], *inputs, total
            )
        else:
            rows = TILE + (hidden if ride else 0)
            (scaled,) = vmem_call(
                pull(False, ride), [((rows, hidden), BF16)], *inputs, *(mixed if ride else [])
            )
    return state, adjoint, weight_grad


def solution(mesh):
    in_specs = (
        P(("row", "col"), None),
        P(("row", "col"), None),
        P(),
        P(("row", "col"), None),
        P(("row", "col")),
        P("row", "col", None, None, None),
        P("row", "col", None),
        P("row", "col", None),
        P("row", "col"),
    )
    out_specs = (P(("row", "col"), None), P(("row", "col"), None), P())

    def whole(*args):
        return per_device(mesh.shape["row"], mesh.shape["col"], *args)

    return jax.shard_map(whole, mesh=mesh, in_specs=in_specs, out_specs=out_specs, check_vma=False)
```

```python
import jax
import jax.numpy as jnp
from jax import lax
from jax.experimental import pallas as pl
from jax.experimental.pallas import tpu as pltpu
from jax.sharding import PartitionSpec as P

TILE = 128
ITERS = 3
ADJOINT = 3
LINE = 4
BF16 = jnp.bfloat16
F32 = jnp.float32
VMEM_LIMIT = 48 * 2**20


def vmem_call(body, outs, *args, spaces=None, scratch=()):
    specs = [pl.BlockSpec(memory_space=space) for space in spaces or [pltpu.VMEM] * len(args)]
    out_specs = [pl.BlockSpec(memory_space=pltpu.VMEM) for _ in outs]
    return pl.pallas_call(
        body,
        out_shape=[jax.ShapeDtypeStruct(shape, dtype) for shape, dtype in outs],
        in_specs=specs,
        out_specs=out_specs,
        scratch_shapes=list(scratch),
        compiler_params=pltpu.CompilerParams(vmem_limit_bytes=VMEM_LIMIT),
    )(*args)


def halves(value):
    high = value.astype(BF16)
    return high, (value - high.astype(F32)).astype(BF16)


def split_dot(value, factor, dims):
    high, low = halves(value)
    return lax.dot_general(high, factor, (dims, ((), ())), preferred_element_type=F32) + lax.dot_general(
        low, factor, (dims, ((), ())), preferred_element_type=F32
    )


def tree_sum(values):
    while len(values) > 1:
        values = [values[i] + values[i + 1] for i in range(0, len(values), 2)]
    return values[0]


def per_device(n_row, n_col, *args):
    anchor, injection, weight, cotangent, node_mask, tile_values, tile_rows, tile_cols, tile_counts = args
    own, hidden = anchor.shape
    assert own == TILE
    slots = tile_values.shape[2]
    z_step = n_row // LINE
    n_y = z_step // 2
    square = [(y, x) for y in range(n_y) for x in range(n_col)]
    line_rows = LINE * TILE
    block = (TILE, hidden)
    where = jnp.stack([lax.axis_index("row"), lax.axis_index("col")]).astype(jnp.int32)

    def exchange(value, row_xor, col_xor=0):
        if col_xor == 0:
            return lax.ppermute(value, "row", [(i, i ^ row_xor) for i in range(n_row)])
        if row_xor == 0:
            return lax.ppermute(value, "col", [(i, i ^ col_xor) for i in range(n_col)])
        pairs = [
            (r * n_col + c, (r ^ row_xor) * n_col + (c ^ col_xor))
            for r in range(n_row)
            for c in range(n_col)
        ]
        return lax.ppermute(value, ("row", "col"), pairs)

    def along_line(values):
        return [exchange(v, z * z_step) for z, v in zip(range(1, LINE), values)]

    def to_square(values):
        return [exchange(v, 2 * y, x) for (y, x), v in zip(square[1:], values)]

    chunk = min(8, slots)
    n_chunks = slots // chunk
    assert slots % chunk == 0

    def build(where_ref, count, *refs):
        small_hbm, tiles_hbm, refs = refs[:5], refs[5], refs[6:]
        parts, turned, fixed_out = refs[:n_y], refs[n_y], refs[n_y + 1]
        small, (tiles, acc, small_sem, tile_sem) = refs[n_y + 2 : n_y + 7], refs[n_y + 7 :]
        rows, cols, inject, cotan, mask = small
        copies = [
            pltpu.make_async_copy(source, target, small_sem.at[i])
            for i, (source, target) in enumerate(zip(small_hbm, small))
        ]
        pieces = [slice(c * chunk, (c + 1) * chunk) for c in range(n_chunks)]
        loads = [
            pltpu.make_async_copy(tiles_hbm.at[0, 0, piece], tiles.at[piece], tile_sem.at[c])
            for c, piece in enumerate(pieces)
        ]
        for copy in copies + loads:
            copy.start()
        acc[...] = jnp.zeros_like(acc)
        for copy in copies:
            copy.wait()
        fixed_out[:TILE] = inject[...]
        kept_nodes = jnp.broadcast_to(mask[...].astype(F32), (TILE, TILE)).T[:, :1]
        fixed_out[TILE:] = (cotan[...].astype(F32) * kept_nodes).astype(BF16)

        def add(k, carry):
            s = cols[0, 0, k] ^ where_ref[0]
            x = rows[0, 0, k] ^ where_ref[1]
            y = (s // 2) % n_y
            acc[((y * n_col + x) * 2 + s % 2) * LINE + s // z_step] += tiles[k].astype(F32)
            return carry

        for c, load in enumerate(loads):
            load.wait()
            lax.fori_loop(c * chunk, jnp.clip(count[0, 0], c * chunk, (c + 1) * chunk), add, 0)
        for y in range(n_y):
            for x in range(n_col):
                for p in range(2 * LINE):
                    tile = acc[(y * n_col + x) * 2 * LINE + p]
                    here, there = slice(x * TILE, (x + 1) * TILE), slice(p * TILE, (p + 1) * TILE)
                    parts[y][here, there] = tile.astype(BF16)
                    if y == 0:
                        turned[there, here] = tile.T.astype(BF16)
            if y > 0:
                parts[y][: 2 * TILE, 2 * line_rows :] = fixed_out[...]
                if n_col > 2:
                    parts[y][2 * TILE :, 2 * line_rows :] = jnp.zeros(((n_col - 2) * TILE, hidden), BF16)

    assert n_col >= 2
    part_shape = (n_col * TILE, 2 * line_rows)
    sent_shape = (n_col * TILE, 2 * line_rows + hidden)
    small = (tile_rows, tile_cols, injection, cotangent, node_mask.reshape(1, -1))
    *parts, turned, fixed = vmem_call(
        build,
        [(part_shape, BF16)] + [(sent_shape, BF16)] * (n_y - 1)
        + [(part_shape[::-1], BF16), ((2 * TILE, hidden), BF16)],
        where,
        tile_counts,
        *[pltpu.with_memory_space_constraint(v, pltpu.HBM) for v in (*small, tile_values)],
        spaces=[pltpu.SMEM] * 2 + [pltpu.HBM] * 6,
        scratch=[
            *[pltpu.SMEM(v.shape, v.dtype) for v in small[:2]],
            *[pltpu.VMEM(v.shape, v.dtype) for v in small[2:]],
            pltpu.VMEM((slots, TILE, TILE), BF16),
            pltpu.VMEM((n_y * n_col * 2 * LINE, TILE, TILE), F32),
            pltpu.SemaphoreType.DMA((5,)),
            pltpu.SemaphoreType.DMA((n_chunks,)),
        ],
    )

    def own_product(block_rows, a, side):
        total = None
        for y in range(n_y):
            part = a[y][:, side * line_rows : (side + 1) * line_rows]
            rows = block_rows[y * line_rows : (y + 1) * line_rows]
            product = jnp.dot(part, rows, preferred_element_type=F32)
            total = product if total is None else total + product
        return total

    def first_near(near, *refs):
        refs[n_y][...] = own_product(near, refs[:n_y], 0)

    def first_far(held, far, *refs):
        a, outs = refs[:n_y], refs[n_y:]
        total = held[...] + own_product(far, a, 1)
        for x in range(n_col):
            outs[x][...] = total[x * TILE : (x + 1) * TILE].astype(outs[x].dtype)

    n_square = len(square)
    square_rows = n_square * TILE

    def forward_near(z0, z1, z2, z3, *refs):
        a, out = refs[:n_y], refs[n_y]
        near = jnp.concatenate([z0[...], z1[...], z2[...], z3[...]], axis=0)
        rows = n_col * TILE
        for y in range(n_y):
            out[y * rows : (y + 1) * rows] = jnp.dot(a[y][:, :line_rows], near, preferred_element_type=F32)

    def far_product(held, far, a, y):
        rows = slice(y * n_col * TILE, (y + 1) * n_col * TILE)
        return held[rows] + jnp.dot(a[y][:, line_rows : 2 * line_rows], far[...], preferred_element_type=F32)

    def forward_far(held, far, fixed_ref, *refs):
        a, outs = refs[:n_y], refs[n_y:]
        for y in range(n_y):
            total = far_product(held, far, a, y)
            for x in range(n_col):
                out = outs[y * n_col + x]
                out[:TILE] = total[x * TILE : (x + 1) * TILE].astype(out.dtype)
                if x > 0:
                    out[TILE:] = fixed_ref[...]

    def forward_far_all(held, far, *refs):
        a, (kept, sent) = refs[:n_y], refs[n_y:]
        for y in range(n_y):
            rows = slice(y * n_col * TILE, (y + 1) * n_col * TILE)
            total = far_product(held, far, a, y)
            kept[rows] = total
            sent[rows] = total.astype(BF16)

    def advance(beta, peers):
        def body(*refs):
            sums, (w, anchor_ref, inject, out) = refs[:peers], refs[peers:]
            u = tree_sum([s[:TILE].astype(F32) for s in sums])
            bent = jnp.tanh(split_dot(u, w[...], ((1,), (0,))) + inject[...].astype(F32))
            out[...] = (beta * anchor_ref[...].astype(F32) + (1.0 - beta) * bent).astype(BF16)

        return body

    def meet(kept, *refs):
        got, refs = refs[: n_square - 1], refs[n_square - 1 :]
        by_y, by_x, (w, bent_out, slope_out, u_out, h_out) = refs[0], refs[1 : -5], refs[-5:]
        by_x = iter(by_x)
        fixed = [
            by_y.at[2 * y * TILE : 2 * (y + 1) * TILE] if x == 0 else next(by_x).at[TILE : 3 * TILE]
            for y, x in square
        ]
        u = jnp.concatenate(
            [
                tree_sum(
                    [kept[j * TILE : (j + 1) * TILE]]
                    + [
                        got[i - 1][(i ^ j) * TILE : ((i ^ j) + 1) * TILE].astype(F32)
                        for i in range(1, n_square)
                    ]
                )
                for j in range(n_square)
            ],
            axis=0,
        )
        inject = jnp.concatenate([f[:TILE] for f in fixed], axis=0).astype(F32)
        bent = jnp.tanh(split_dot(u, w[...], ((1,), (0,))) + inject)
        slope = 1.0 - bent * bent
        base = jnp.concatenate([f[TILE:] for f in fixed], axis=0).astype(F32)
        h_out[...] = (base * slope).astype(BF16)
        bent_out[...] = bent[:TILE]
        slope_out[...] = slope[:TILE]
        u_out[...] = u[:TILE]

    def turn(fixed_ref, *refs):
        came, outs, fixed_out = refs[: n_y - 1], refs[n_y - 1 : -1], refs[-1]
        fixed_out[: 2 * TILE] = fixed_ref[...]
        for y in range(1, n_y):
            part, out = came[y - 1], outs[y - 1]
            fixed_out[2 * y * TILE : 2 * (y + 1) * TILE] = part[: 2 * TILE, 2 * line_rows :]
            for x in range(n_col):
                for p in range(2 * LINE):
                    here, there = slice(x * TILE, (x + 1) * TILE), slice(p * TILE, (p + 1) * TILE)
                    out[there, here] = part[here, there].T

    state = anchor
    for step in range(ITERS):
        beta = 1.0 / (step + 2.0)
        line = [state] + along_line([state] * (LINE - 1))
        if step == 0:
            joined = jnp.concatenate(line, axis=0)
            joined, *parts, turned = lax.optimization_barrier((joined, *parts, turned))
            bit = 2
            while bit < z_step:
                joined = jnp.concatenate([joined, exchange(joined, bit)], axis=0)
                bit *= 2
            sent = parts[1:]
            far = exchange(joined, 1)
            (held,) = vmem_call(first_near, [((n_col * TILE, hidden), F32)], joined, *parts)
            outs = [(block, F32)] + [(block, BF16)] * (n_col - 1)
            mine, *sends = vmem_call(first_far, outs, held, far, *parts)
            parts = [parts[0]] + [exchange(p, 2 * (i + 1)) for i, p in enumerate(sent)]
            got = [exchange(v, 0, x + 1) for x, v in enumerate(sends)]
        else:
            far = exchange(jnp.concatenate(line, axis=0), 1)
            (held,) = vmem_call(forward_near, [((square_rows, hidden), F32)], *line, *parts)
            if step == ITERS - 1:
                outs = [((square_rows, hidden), F32), ((square_rows, hidden), BF16)]
                kept, sent = vmem_call(forward_far_all, outs, held, far, *parts)
                got = to_square([sent] * (n_square - 1))
                bent, slope, mixed, h_all = vmem_call(
                    meet, [(block, F32)] * 3 + [((square_rows, hidden), BF16)], kept, *got, fixed_y, *fixed_x, weight
                )
                break
            outs = [(block, F32)] + [((TILE if x == 0 else 3 * TILE, hidden), BF16) for y, x in square[1:]]
            mine, *sends = vmem_call(forward_far, outs, held, far, fixed, *parts)
            got = to_square(sends)
            fixed_x = [v for (y, x), v in zip(square[1:], got) if x > 0]
        if step == 1:
            *more, fixed_y = vmem_call(
                turn,
                [(part_shape[::-1], BF16)] * (n_y - 1) + [((2 * n_y * TILE, hidden), BF16)],
                fixed,
                *parts[1:],
            )
            turned = [turned] + more
        (state,) = vmem_call(
            advance(beta, 1 + len(got)), [(block, BF16)], mine, *got, weight, anchor, injection
        )

    def finish(bent_ref, anchor_ref, u, out, high, low):
        out[...] = (beta * anchor_ref[...].astype(F32) + (1.0 - beta) * bent_ref[...]).astype(BF16)
        high[...], low[...] = halves(u[...].T)

    state, *mixed = vmem_call(
        finish, [(block, BF16)] + [((hidden, TILE), BF16)] * 2, bent, anchor, mixed
    )

    def line_product(h, a_t, rows):
        total = None
        for y in range(n_y):
            if len(h) == 1:
                joined = h[0][y * n_col * TILE : (y + 1) * n_col * TILE]
            else:
                joined = jnp.concatenate([h[y * n_col + x][:TILE] for x in range(n_col)], axis=0)
            product = jnp.dot(a_t[y][rows], joined, preferred_element_type=F32)
            total = product if total is None else total + product
        return total

    def backward_near(n):
        def body(*refs):
            refs[-1][...] = line_product(refs[:n], refs[n:-1], slice(0, line_rows))

        return body

    def backward_far(n, last):
        def body(*refs):
            h, a_t, (far, *term) = refs[:n], refs[n : n + n_y], refs[n + n_y :]
            far[:line_rows] = line_product(h, a_t, slice(line_rows, 2 * line_rows)).astype(BF16)
            if last:
                whole = tree_sum([v[TILE:].astype(F32) for v in h])
                high, low = halves(whole)
                far[line_rows : line_rows + hidden] = high
                far[line_rows + hidden :] = low
                term[0][...] = high.astype(F32) + low.astype(F32)

        return body

    def fold(last):
        def body(held, got, *refs):
            outs = refs[1:] if last else refs
            for z in range(LINE):
                rows = slice(z * TILE, (z + 1) * TILE)
                value = held[rows] + got[rows].astype(F32)
                if z == 0:
                    outs[0][...] = value
                else:
                    outs[z][:TILE] = value.astype(BF16)
            if last:
                high, low = got[line_rows : line_rows + hidden], got[line_rows + hidden :]
                term = (refs[0][...] + (high.astype(F32) + low.astype(F32))).astype(BF16)
                outs[LINE][...] = term.astype(F32)
                for z in range(1, LINE):
                    outs[z][TILE:] = term

        return body

    def pull(last, ride):
        def body(held, *refs):
            got, rest = refs[: LINE - 1], refs[LINE - 1 :]
            v = tree_sum([held[...]] + [r[:TILE].astype(F32) for r in got])
            base, w, slope_ref = rest[:3]
            g = base[TILE : 2 * TILE].astype(F32) + split_dot(v, w[...], ((1,), (1,)))
            if last:
                term, adjoint_out, grad_out = rest[3:]
                adjoint_out[...] = g
                whole = tree_sum([term[...]] + [r[TILE:].astype(F32) for r in got])
                grad_out[...] = whole / (own * n_col)
            else:
                out = rest[-1]
                h = (g * slope_ref[...]).astype(BF16)
                out[:TILE] = h
                if ride:
                    term = jnp.dot(rest[3][...], h, preferred_element_type=F32)
                    term += jnp.dot(rest[4][...], h, preferred_element_type=F32)
                    out[TILE:] = term.astype(BF16)

        return body

    for step in range(ADJOINT):
        last, ride = step == ADJOINT - 1, step == ADJOINT - 2
        states = [h_all] if step == 0 else [scaled] + to_square([scaled] * (n_square - 1))
        extra = 2 * hidden if last else 0
        far, *term = vmem_call(
            backward_far(len(states), last),
            [((line_rows + extra, hidden), BF16)] + ([((hidden, hidden), F32)] if last else []),
            *states,
            *turned,
        )
        (near,) = vmem_call(
            backward_near(len(states)), [((line_rows, hidden), F32)], *states, *turned
        )
        got = exchange(far, 1)
        extra = hidden if last else 0
        held, *sends = vmem_call(
            fold(last),
            [(block, F32)]
            + [((TILE + extra, hidden), BF16)] * (LINE - 1)
            + ([((hidden, hidden), F32)] if last else []),
            near,
            got,
            *term,
        )
        if last:
            *sends, total = sends
        got = along_line(sends)
        inputs = (held, *got, fixed, weight, slope)
        if last:
            adjoint, weight_grad = vmem_call(
                pull(True, False), [(block, F32), ((hidden, hidden), F32)], *inputs, total
            )
        else:
            rows = TILE + (hidden if ride else 0)
            (scaled,) = vmem_call(
                pull(False, ride), [((rows, hidden), BF16)], *inputs, *(mixed if ride else [])
            )
    return state, adjoint, weight_grad


def solution(mesh):
    in_specs = (
        P(("row", "col"), None),
        P(("row", "col"), None),
        P(),
        P(("row", "col"), None),
        P(("row", "col")),
        P("row", "col", None, None, None),
        P("row", "col", None),
        P("row", "col", None),
        P("row", "col"),
    )
    out_specs = (P(("row", "col"), None), P(("row", "col"), None), P())

    def whole(*args):
        return per_device(mesh.shape["row"], mesh.shape["col"], *args)

    return jax.shard_map(whole, mesh=mesh, in_specs=in_specs, out_specs=out_specs, check_vma=False)
```
